32 devices in a mesh: seq: 8 (over z, y), head: 4 (over x, core).
Axes of the slice: x: 2, y: 2, z: 4, core: 2. Of those that a mesh axis runs over, the one named last changes fastest.
Arguments:
- queries: bfloat16 [4096, 2048], P(('seq', 'head')), may hold values from -6 to 6
- output_gradient: bfloat16 [4096, 2048], P(('seq', 'head')), may hold values from -6 to 6
- outputs: bfloat16 [4096, 2048], P(('seq', 'head')), may hold values from -6 to 6
- key_vectors: bfloat16 [4096, 1024], P(('seq', 'head')), may hold values from -6 to 6
- values: bfloat16 [4096, 1024], P(('seq', 'head')), may hold values from -6 to 6
- logsum: float32 [16, 4096], P('head', 'seq'), as said below
- pair_list: int32 [20, 3], replicated, may hold values from 0 to 7, as said below
Outputs:
- grad_queries: bfloat16 [4096, 2048], P(('seq', 'head'))
- key_gradient: bfloat16 [4096, 1024], P(('seq', 'head'))
- value_gradient: bfloat16 [4096, 1024], P(('seq', 'head'))
The draws below stay inside these ranges and needn't reach their ends.
Inputs may be any that keep to these rules, and one draw needn't show every extreme that they name: `pair_list`: every block b has the row (b, b, 1). Every other row (a, c, m) has 1 <= a - c <= 4 and m equal to 0 or 2. No pair appears twice; rows come in no particular order. A query block has between 1 and 5 rows, and block 7 has 5. `logsum`: each entry lies between ln(512) + 0.5 and ln(2560) + 0.5.
All inputs are finite; a program needn't handle non-finite values.
Results may differ from the reference program's by a relative error of at most 0.0054.
Values may be sent and summed in bfloat16 or wider, within the bound.
No kernel may reach another device: no remote copies, remote signals or barrier semaphores. Data moves between devices by JAX's collectives and lax.ppermute only.
A program may use at most 64 MiB of HBM per device.

```python
import jax
import jax.numpy as jnp
from jax import lax

HEAD_SIZE = 128
KEY_VALUE_HEADS = 8
QUERY_HEADS = 16
BLOCK_TOKENS = 512
WIN = 5
BLOCK_COUNT = 8
SEQUENCE_TOKENS = 4096
PAIRS = 20


def draw_logsum(key, part):
    low_end = jnp.log(jnp.float32(BLOCK_TOKENS)) + 0.5
    spread = jnp.log(jnp.float32(WIN))
    level = jax.random.uniform(jax.random.fold_in(key, 21), (QUERY_HEADS, SEQUENCE_TOKENS), jnp.float32)
    return (low_end + spread * level).astype(jnp.float32)


def draw_pair_list(key, part):
    cand_count = BLOCK_COUNT * (WIN - 1)
    extra = 3 * (BLOCK_COUNT - 4)
    blocks = jnp.repeat(jnp.arange(BLOCK_COUNT, dtype=jnp.int32), WIN - 1)
    offsets = jnp.tile(jnp.arange(1, WIN, dtype=jnp.int32), BLOCK_COUNT)
    valid = blocks - offsets >= 0
    random_bits = jax.random.randint(jax.random.fold_in(key, 11), (cand_count,), 0, 1 << 20)
    ranking = jnp.where(valid, random_bits + 2, 0)
    ranking = jnp.where(blocks == BLOCK_COUNT - 1, (1 << 20) + 2, ranking)
    ranking = ranking * cand_count + jnp.arange(cand_count, dtype=jnp.int32)
    picked = jnp.argsort(-ranking)[:extra]
    kinds = jax.random.randint(jax.random.fold_in(key, 12), (extra,), 0, 2) * 2
    extra_rows = jnp.stack([blocks[picked], blocks[picked] - offsets[picked], kinds], axis=1)
    diag_ids = jnp.arange(BLOCK_COUNT, dtype=jnp.int32)
    diag_rows = jnp.stack([diag_ids, diag_ids, jnp.ones((BLOCK_COUNT,), jnp.int32)], axis=1)
    all_rows = jnp.concatenate([diag_rows, extra_rows], axis=0)
    shuffle = jax.random.permutation(jax.random.fold_in(key, 13), PAIRS)
    return all_rows[shuffle].astype(jnp.int32)


def levels(own_key, extent, shards, smallest, high):
    def one(axis_at, shards_of):
        heights = jax.random.uniform(jax.random.fold_in(jax.random.fold_in(own_key, 6), axis_at), (shards_of,), jnp.float32, smallest / len(shards), high / len(shards))
        return jnp.repeat(jnp.exp(heights), extent[axis_at] // shards_of).reshape((-1,) + (1,) * (len(extent) - axis_at - 1))

    level = one(*shards[0])
    for cut in shards[1:]:
        level = level * one(*cut)
    return level


def noise(stream_key, dims, scale, most, split=(), kind=jnp.bfloat16):
    array = jax.random.normal(stream_key, dims, jnp.float32) * scale
    if len(split) > 0:
        array = levels(stream_key, dims, split, -0.22, 0.18) * array
    return jnp.clip(array, min=-most, max=most).astype(kind)


def setup_inputs(seed: int = 0) -> dict:
    streams_of = jax.random.split(jax.random.key(seed), 8)
    return {
        "queries": noise(streams_of[0], (SEQUENCE_TOKENS, QUERY_HEADS * HEAD_SIZE), 1.0, 6.0, ((0, 32),)),
        "output_gradient": noise(streams_of[1], (SEQUENCE_TOKENS, QUERY_HEADS * HEAD_SIZE), 1.0, 6.0, ((0, 32),)),
        "outputs": noise(streams_of[2], (SEQUENCE_TOKENS, QUERY_HEADS * HEAD_SIZE), 1.0, 6.0, ((0, 32),)),
        "key_vectors": noise(streams_of[3], (SEQUENCE_TOKENS, KEY_VALUE_HEADS * HEAD_SIZE), 1.0, 6.0, ((0, 32),)),
        "values": noise(streams_of[4], (SEQUENCE_TOKENS, KEY_VALUE_HEADS * HEAD_SIZE), 1.0, 6.0, ((0, 32),)),
        "logsum": draw_logsum(jax.random.fold_in(streams_of[7], 71), 0),
        "pair_list": draw_pair_list(jax.random.fold_in(streams_of[7], 71), 0),
    }


def block_grads(q_block, do_block, lse_block, delta_block, k_block, v_block, pair_code):
    score_scale = 1.0 / jnp.sqrt(jnp.float32(HEAD_SIZE))
    q_float = q_block.astype(jnp.float32)
    do_float = do_block.astype(jnp.float32)
    k_float = k_block.astype(jnp.float32)
    v_float = v_block.astype(jnp.float32)
    scores = jnp.einsum('qkgd,skd->kgqs', q_float, k_float) * score_scale
    row_ids = jnp.arange(BLOCK_TOKENS)[:, None]
    col_ids = jnp.arange(BLOCK_TOKENS)[None, :]
    allowed = (pair_code == 1) | (pair_code == 2) & (col_ids <= row_ids) | (pair_code == 3) & (col_ids > row_ids)
    probs = jnp.where(allowed, jnp.exp(scores - lse_block[..., None]), jnp.float32(0.0))
    probs_low = probs.astype(jnp.bfloat16).astype(jnp.float32)
    grad_v = jnp.einsum('kgqs,qkgd->skd', probs_low, do_float)
    dprobs = jnp.einsum('qkgd,skd->kgqs', do_float, v_float)
    dscores = (probs * (dprobs - delta_block[..., None]) * score_scale).astype(jnp.bfloat16).astype(jnp.float32)
    grad_q = jnp.einsum('kgqs,skd->qkgd', dscores, k_float)
    grad_k = jnp.einsum('kgqs,qkgd->skd', dscores, q_float)
    return (grad_q, grad_k, grad_v)

def reference(queries, output_gradient, outputs, key_vectors, values, logsum, pair_list):
    group_count = QUERY_HEADS // KEY_VALUE_HEADS
    query_every_row = queries.reshape(BLOCK_COUNT, BLOCK_TOKENS, KEY_VALUE_HEADS, group_count, HEAD_SIZE)
    output_grad_rows = output_gradient.reshape(BLOCK_COUNT, BLOCK_TOKENS, KEY_VALUE_HEADS, group_count, HEAD_SIZE)
    key_every_row = key_vectors.reshape(BLOCK_COUNT, BLOCK_TOKENS, KEY_VALUE_HEADS, HEAD_SIZE)
    value_every_row = values.reshape(BLOCK_COUNT, BLOCK_TOKENS, KEY_VALUE_HEADS, HEAD_SIZE)
    delta_term = lax.optimization_barrier(jnp.sum(output_gradient.astype(jnp.float32).reshape(SEQUENCE_TOKENS, QUERY_HEADS, HEAD_SIZE) * outputs.astype(jnp.float32).reshape(SEQUENCE_TOKENS, QUERY_HEADS, HEAD_SIZE), axis=-1))
    delta_every_row = delta_term.reshape(BLOCK_COUNT, BLOCK_TOKENS, KEY_VALUE_HEADS, group_count).transpose(0, 2, 3, 1)
    logsumexp_rows = logsum.reshape(KEY_VALUE_HEADS, group_count, BLOCK_COUNT, BLOCK_TOKENS).transpose(2, 0, 1, 3)

    def one_pair(carry, pair_row):
        acc_q, key_grad_total, value_grad_total = carry
        q_index = pair_row[0]
        k_index = pair_row[1]
        grad_q, grad_k, grad_v = block_grads(query_every_row[q_index], output_grad_rows[q_index], logsumexp_rows[q_index], delta_every_row[q_index], key_every_row[k_index], value_every_row[k_index], pair_row[2] + 1)
        acc_q = acc_q.at[q_index].add(grad_q)
        key_grad_total = key_grad_total.at[k_index].add(grad_k)
        value_grad_total = value_grad_total.at[k_index].add(grad_v)
        return ((acc_q, key_grad_total, value_grad_total), None)
    start_offset = (jnp.zeros((BLOCK_COUNT, BLOCK_TOKENS, KEY_VALUE_HEADS, group_count, HEAD_SIZE), jnp.float32), jnp.zeros((BLOCK_COUNT, BLOCK_TOKENS, KEY_VALUE_HEADS, HEAD_SIZE), jnp.float32), jnp.zeros((BLOCK_COUNT, BLOCK_TOKENS, KEY_VALUE_HEADS, HEAD_SIZE), jnp.float32))
    (acc_q, key_grad_total, value_grad_total), _ = lax.scan(one_pair, start_offset, pair_list)
    grad_queries = acc_q.reshape(SEQUENCE_TOKENS, QUERY_HEADS * HEAD_SIZE).astype(jnp.bfloat16)
    key_gradient = key_grad_total.reshape(SEQUENCE_TOKENS, KEY_VALUE_HEADS * HEAD_SIZE).astype(jnp.bfloat16)
    value_gradient = value_grad_total.reshape(SEQUENCE_TOKENS, KEY_VALUE_HEADS * HEAD_SIZE).astype(jnp.bfloat16)
    return (grad_queries, key_gradient, value_gradient)
```

```python
import functools
import math

import jax
import jax.numpy as jnp
from jax import lax
from jax.experimental import pallas as pl
from jax.experimental.pallas import tpu as pltpu
from jax.sharding import Mesh, PartitionSpec as P

HEAD_SIZE = 128
KEY_VALUE_HEADS = 8
QUERY_HEADS = 16
WIN = 5
GROUP = QUERY_HEADS // KEY_VALUE_HEADS
TILE = 256
AUX = 16
LANES = 128
LOG2E = math.log2(math.e)
SCALE = 1.0 / math.sqrt(HEAD_SIZE)
BF16 = jnp.bfloat16
F32 = jnp.float32
CROSS = ("y", "head")
WHOLE = pl.BlockSpec(memory_space=pltpu.VMEM)
SCALARS = pl.BlockSpec(memory_space=pltpu.SMEM)
VMEM_BYTES = 48 * 1024 * 1024


def call(kernel, out_shape, in_specs, name, flops=0, moved=4 << 20, scratch=()):
    return pl.pallas_call(
        kernel,
        out_shape=out_shape,
        in_specs=in_specs,
        out_specs=jax.tree.map(lambda _: WHOLE, out_shape),
        scratch_shapes=scratch,
        name=name,
        cost_estimate=pl.CostEstimate(flops=flops, bytes_accessed=moved, transcendentals=0),
        compiler_params=pltpu.CompilerParams(vmem_limit_bytes=VMEM_BYTES),
    )


def split3(x):
    hi = x.astype(BF16)
    rest = x - hi.astype(F32)
    mid = rest.astype(BF16)
    low = (rest - mid.astype(F32)).astype(BF16)
    return hi, mid, low


def padded_lanes(x):
    rows, width = x.shape
    if width == LANES:
        return x
    return jnp.concatenate([x, jnp.zeros((rows, LANES - width), x.dtype)], axis=1)


def head_of(member, fold, n_head):
    return (member % n_head) * fold + member // n_head


def pack_q_kernel(fold, n_head, me_ref, q_ref, do_ref, o_ref, *refs):
    members = fold * n_head
    pieces, (delta_ref,) = refs[:members], refs[members:]
    tokens = q_ref.shape[0]
    sums = []
    for head in range(QUERY_HEADS):
        cols = slice(head * HEAD_SIZE, (head + 1) * HEAD_SIZE)
        product = do_ref[:, cols].astype(F32) * o_ref[:, cols].astype(F32)
        sums.append(jnp.sum(product, axis=1, keepdims=True))
    sums.append(jnp.zeros((tokens, LANES - QUERY_HEADS), F32))
    delta_ref[...] = padded_lanes(jnp.concatenate(sums, axis=1).T)
    for mask in range(members):
        kv_head = head_of(me_ref[0] ^ mask, fold, n_head)
        out = pieces[mask]
        for g in range(GROUP):
            cols = pl.ds(pl.multiple_of((kv_head * GROUP + g) * HEAD_SIZE, LANES), HEAD_SIZE)
            out[g * tokens : (g + 1) * tokens, :] = q_ref[:, cols]
            out[(GROUP + g) * tokens : (GROUP + g + 1) * tokens, :] = do_ref[:, cols]
        rows = [delta_ref[pl.ds(kv_head * GROUP + g, 1), :] for g in range(GROUP)]
        terms = [term for row in rows for term in split3(row)]
        terms.append(jnp.zeros((AUX - len(terms), LANES), BF16))
        out[2 * GROUP * tokens :, :] = jnp.concatenate(terms, axis=0)


def pack_kv_kernel(fold, n_head, me_ref, k_ref, v_ref, *pieces):
    tokens = k_ref.shape[0]
    for mask, out in enumerate(pieces):
        kv_head = head_of(me_ref[0] ^ mask, fold, n_head)
        cols = pl.ds(pl.multiple_of(kv_head * HEAD_SIZE, LANES), HEAD_SIZE)
        out[:tokens, :] = k_ref[:, cols]
        out[tokens:, :] = v_ref[:, cols]


def assemble_q_kernel(fold, n_head, me_ref, lse_ref, *refs):
    members = fold * n_head
    pieces, (q_out,) = refs[:members], refs[members:]
    tokens = (pieces[0].shape[0] - AUX) // (2 * GROUP)
    body = 2 * GROUP * tokens
    for mask in range(members):
        member = me_ref[0] ^ mask
        q_out[member, :body, :] = pieces[mask][:body, :]
    for mask in range(members):
        member = me_ref[0] ^ mask
        terms = [pieces[mask][body : body + 3 * GROUP, :]]
        for g in range(GROUP):
            terms.extend(split3(lse_ref[member, pl.ds(g, 1), :]))
        terms.append(jnp.zeros((AUX - 6 * GROUP, LANES), BF16))
        q_out[member, body:, :] = jnp.concatenate(terms, axis=0)


def assemble_kv_kernel(me_ref, *refs):
    pieces, kv_out = refs[:-1], refs[-1]
    for mask, piece in enumerate(pieces):
        kv_out[me_ref[0] ^ mask] = piece[...]


def lane_row(parts, tokens):
    if tokens == LANES:
        return jnp.concatenate(parts, axis=1)
    per = LANES // tokens
    lane = lax.broadcasted_iota(jnp.int32, (1, LANES), 1)
    out = []
    for start in range(0, len(parts), per):
        row = parts[start]
        for k in range(1, per):
            moved = pltpu.roll(parts[start + k], k * tokens, 1)
            row = jnp.where(lane >= k * tokens, moved, row)
        out.append(row)
    return jnp.concatenate(out, axis=1)


def role_kernel(fold, n_head, has_dq, has_dkv, code_ref, q_ref, kv_ref, *refs):
    refs = list(refs)
    dq_in = refs.pop(0) if has_dq else None
    dkv_in = refs.pop(0) if has_dkv else None
    dq_out, dkv_out, dq_ref, dkv_ref = refs
    tokens = kv_ref.shape[1] // 2
    block = n_head * tokens
    tiles = block // TILE
    chunks = TILE // tokens
    dq_ref[...] = dq_in[...] if has_dq else jnp.zeros_like(dq_ref)
    dkv_ref[...] = dkv_in[...] if has_dkv else jnp.zeros_like(dkv_ref)

    def one_tile(q_tile, k_tile, code, masked):
        q_chunk = q_tile * chunks
        k_chunk = k_tile * chunks

        def q_rows(which):
            return jnp.concatenate(
                [
                    q_ref[q_chunk + n, (which * GROUP + g) * tokens : (which * GROUP + g + 1) * tokens, :]
                    for g in range(GROUP)
                    for n in range(chunks)
                ],
                axis=0,
            )

        def aux(which):
            base = 2 * GROUP * tokens
            parts = []
            for g in range(GROUP):
                row = base + (which * GROUP + g) * 3
                for n in range(chunks):
                    group = q_ref[q_chunk + n, base : base + AUX, :].astype(F32)
                    at = row - base
                    parts.append(group[at : at + 1] + group[at + 1 : at + 2] + group[at + 2 : at + 3])
            return lane_row(parts, tokens)

        q2, do2 = q_rows(0), q_rows(1)
        delta, lse = aux(0), aux(1)
        k = jnp.concatenate([kv_ref[k_chunk + n, :tokens, :] for n in range(chunks)], axis=0)
        v = jnp.concatenate([kv_ref[k_chunk + n, tokens:, :] for n in range(chunks)], axis=0)
        last = (((1,), (1,)), ((), ()))
        scores = lax.dot_general(k, q2, last, preferred_element_type=F32)
        dprobs = lax.dot_general(v, do2, last, preferred_element_type=F32)
        probs = jnp.exp2(scores * (SCALE * LOG2E) - lse * LOG2E)
        if masked:
            key_id = lax.broadcasted_iota(jnp.int32, probs.shape, 0)
            query_id = lax.broadcasted_iota(jnp.int32, probs.shape, 1) % TILE
            ahead = key_id - query_id
            allowed = jnp.where(code == 2, ahead, 1 - ahead) <= 0
            probs = jnp.where(allowed, probs, 0.0)
        dscores = (probs * (dprobs - delta) * SCALE).astype(BF16)
        low = probs.astype(BF16)
        dv = jnp.dot(low, do2, preferred_element_type=F32)
        dk = jnp.dot(dscores, q2, preferred_element_type=F32)
        dq_ref[q_tile] += jnp.dot(k.T, dscores, preferred_element_type=F32)
        for n in range(chunks):
            rows = slice(n * tokens, (n + 1) * tokens)
            dkv_ref[k_chunk + n, :tokens, :] += dk[rows]
            dkv_ref[k_chunk + n, tokens:, :] += dv[rows]

    def step(index, carry):
        k_in = index % tiles
        q_in = (index // tiles) % tiles
        key_block = (index // (tiles * tiles)) % fold
        query_block = index // (tiles * tiles * fold)
        code = code_ref[query_block, key_block]
        plain = (code == 1) | ((code == 2) & (k_in < q_in)) | ((code == 3) & (k_in > q_in))
        cut = (code >= 2) & (k_in == q_in)
        q_tile = query_block * tiles + q_in
        k_tile = key_block * tiles + k_in

        @pl.when(plain)
        def _():
            one_tile(q_tile, k_tile, code, False)

        @pl.when(cut)
        def _():
            one_tile(q_tile, k_tile, code, True)

        return carry

    lax.fori_loop(0, fold * fold * tiles * tiles, step, 0)
    dq_out[...] = dq_ref[...].astype(dq_out.dtype)
    dkv_out[...] = dkv_ref[...].astype(dkv_out.dtype)


def finish_kernel(has_dq, has_dkv, me_ref, dq_ref, dkv_ref, *refs):
    refs = list(refs)
    dq_far = refs.pop(0) if has_dq else None
    dkv_far = refs.pop(0) if has_dkv else None
    pieces, (rows_ref,) = refs[:-1], refs[-1:]
    tokens = dkv_ref.shape[1] // 2
    chunks = TILE // tokens
    for tile in range(dq_ref.shape[0]):
        total = dq_ref[tile]
        if has_dq:
            total = total + dq_far[tile].astype(F32)
        for g in range(GROUP):
            turned = total[:, g * TILE : (g + 1) * TILE].T
            for n in range(chunks):
                rows_ref[tile * chunks + n, g * tokens : (g + 1) * tokens, :] = turned[
                    n * tokens : (n + 1) * tokens
                ].astype(BF16)
    for mask, out in enumerate(pieces):
        member = me_ref[0] ^ mask
        total = dkv_ref[member]
        if has_dkv:
            total = total + dkv_far[member].astype(F32)
        out[: GROUP * tokens, :] = rows_ref[member]
        out[GROUP * tokens :, :] = total.astype(BF16)


def unpack_kernel(fold, n_head, me_ref, *refs):
    members = fold * n_head
    pieces = refs[:members]
    dq_ref, dk_ref, dv_ref = refs[members:]
    tokens = dk_ref.shape[0]
    for mask, piece in enumerate(pieces):
        kv_head = head_of(me_ref[0] ^ mask, fold, n_head)
        for g in range(GROUP):
            cols = pl.ds(pl.multiple_of((kv_head * GROUP + g) * HEAD_SIZE, LANES), HEAD_SIZE)
            dq_ref[:, cols] = piece[g * tokens : (g + 1) * tokens, :]
        cols = pl.ds(pl.multiple_of(kv_head * HEAD_SIZE, LANES), HEAD_SIZE)
        dk_ref[:, cols] = piece[GROUP * tokens : (GROUP + 1) * tokens, :]
        dv_ref[:, cols] = piece[(GROUP + 1) * tokens :, :]


def exchange(pieces):
    members = len(pieces)
    return [pieces[0]] + [
        lax.ppermute(pieces[mask], CROSS, [(i, i ^ mask) for i in range(members)])
        for mask in range(1, members)
    ]


def along(value, planes, steps):
    pairs = [(i, i + steps) for i in range(planes) if 0 <= i + steps < planes]
    return lax.ppermute(value, "z", pairs)


def shards(queries, output_gradient, outputs, key_vectors, values, logsum, pair_list):
    planes, fold, n_head = (lax.axis_size(a) for a in ("z", "y", "head"))
    members = fold * n_head
    tokens = queries.shape[0]
    block = n_head * tokens
    q_tiles = fold * (block // TILE)
    reach = -(-(WIN - 1) // fold)
    y = lax.axis_index("y")
    z = lax.axis_index("z")
    me = (y * n_head + lax.axis_index("head")).astype(jnp.int32).reshape(1)

    q_piece = jax.ShapeDtypeStruct((2 * GROUP * tokens + AUX, LANES), BF16)
    kv_piece = jax.ShapeDtypeStruct((2 * tokens, LANES), BF16)
    q_pieces = call(
        functools.partial(pack_q_kernel, fold, n_head),
        [q_piece] * members,
        [SCALARS, WHOLE, WHOLE, WHOLE],
        "pack_q",
        scratch=[pltpu.VMEM((LANES, LANES), F32)],
    )(me, queries, output_gradient, outputs)
    kv_pieces = call(
        functools.partial(pack_kv_kernel, fold, n_head),
        [kv_piece] * members,
        [SCALARS, WHOLE, WHOLE],
        "pack_kv",
    )(me, key_vectors, values)

    lse_rows = logsum.reshape(fold, GROUP, block)
    lse_parts = [
        lax.ppermute(
            lax.dynamic_index_in_dim(lse_rows, y ^ mask, 0, keepdims=False),
            "y",
            [(i, i ^ mask) for i in range(fold)],
        )
        if mask
        else lax.dynamic_index_in_dim(lse_rows, y, 0, keepdims=False)
        for mask in range(fold)
    ]
    lse = jnp.stack([lax.select_n(y == 0, lse_parts[fold - 1 - b], lse_parts[b]) for b in range(fold)]) if fold > 1 else lse_parts[0][None]
    lse = lse.reshape(fold, GROUP, n_head, tokens).transpose(0, 2, 1, 3).reshape(members, GROUP, tokens)
    if tokens < LANES:
        lse = jnp.pad(lse, ((0, 0), (0, 0), (0, LANES - tokens)))

    q_own = call(
        functools.partial(assemble_q_kernel, fold, n_head),
        jax.ShapeDtypeStruct((members,) + q_piece.shape, BF16),
        [SCALARS] + [WHOLE] * (members + 1),
        "assemble_q",
    )(me, lse, *exchange(q_pieces))
    kv_own = call(
        assemble_kv_kernel,
        jax.ShapeDtypeStruct((members,) + kv_piece.shape, BF16),
        [SCALARS] + [WHOLE] * members,
        "assemble_kv",
    )(me, *exchange(kv_pieces))

    up = [kv_own]
    down = [q_own]
    for _ in range(reach // 2):
        down.append(along(down[-1], planes, -1))
    for _ in range((reach + 1) // 2):
        up.append(along(up[-1], planes, 1))

    grad_q = [None] * len(down)
    grad_kv = [None] * len(up)
    dq_shape = (q_tiles, HEAD_SIZE, GROUP * TILE)
    dkv_shape = (members, 2 * tokens, HEAD_SIZE)
    inside = jnp.arange(fold, dtype=jnp.int32)
    for distance in range(reach + 1):
        i, j = (distance + 1) // 2, distance // 2
        query_blocks = (z + j) * fold + inside
        key_blocks = (z - i) * fold + inside
        hit = (pair_list[:, 0, None, None] == query_blocks[None, :, None]) & (
            pair_list[:, 1, None, None] == key_blocks[None, None, :]
        )
        codes = jnp.sum(jnp.where(hit, pair_list[:, 2, None, None] + 1, 0), axis=0).astype(jnp.int32)
        last_q = distance == min(2 * j + 1, reach)
        last_kv = distance == min(2 * i, reach)
        has_dq, has_dkv = grad_q[j] is not None, grad_kv[i] is not None
        carried = [g for g in (grad_q[j], grad_kv[i]) if g is not None]
        grad_q[j], grad_kv[i] = call(
            functools.partial(role_kernel, fold, n_head, has_dq, has_dkv),
            [
                jax.ShapeDtypeStruct(dq_shape, BF16 if last_q and j else F32),
                jax.ShapeDtypeStruct(dkv_shape, BF16 if last_kv and i else F32),
            ],
            [SCALARS] + [WHOLE] * (2 + len(carried)),
            f"role_{i}_{j}",
            flops=10 * fold * fold * GROUP * block * block * HEAD_SIZE,
            scratch=[pltpu.VMEM(dq_shape, F32), pltpu.VMEM(dkv_shape, F32)],
        )(codes, down[j], up[i], *carried)

    def gathered(parts, step):
        far = None
        for level in range(len(parts) - 1, 0, -1):
            part = parts[level]
            if far is not None:
                part = (part.astype(F32) + far.astype(F32)).astype(BF16)
            far = along(part, planes, step)
        return far

    far_q = gathered(grad_q, 1)
    far_kv = gathered(grad_kv, -1)
    far = [f for f in (far_q, far_kv) if f is not None]
    out_piece = jax.ShapeDtypeStruct(((GROUP + 2) * tokens, LANES), BF16)
    out_pieces = call(
        functools.partial(finish_kernel, far_q is not None, far_kv is not None),
        [out_piece] * members,
        [SCALARS] + [WHOLE] * (2 + len(far)),
        "finish",
        scratch=[pltpu.VMEM((members, GROUP * tokens, LANES), BF16)],
    )(me, grad_q[0], grad_kv[0], *far)
    return tuple(
        call(
            functools.partial(unpack_kernel, fold, n_head),
            [
                jax.ShapeDtypeStruct((tokens, QUERY_HEADS * HEAD_SIZE), BF16),
                jax.ShapeDtypeStruct((tokens, KEY_VALUE_HEADS * HEAD_SIZE), BF16),
                jax.ShapeDtypeStruct((tokens, KEY_VALUE_HEADS * HEAD_SIZE), BF16),
            ],
            [SCALARS] + [WHOLE] * members,
            "unpack",
        )(me, *exchange(out_pieces))
    )


def solution(mesh):
    n_seq, n_head = mesh.shape["seq"], mesh.shape["head"]
    fold = KEY_VALUE_HEADS // n_head
    assert n_head * fold == KEY_VALUE_HEADS and n_seq % fold == 0
    planes = Mesh(mesh.devices.reshape(n_seq // fold, fold, n_head), ("z", "y", "head"))
    rows = P(("z", "y", "head"), None)
    return jax.shard_map(
        shards,
        mesh=planes,
        in_specs=(rows,) * 5 + (P("head", ("z", "y")), P()),
        out_specs=(rows,) * 3,
        check_vma=False,
    )
```

```python
import functools
import math

import jax
import jax.numpy as jnp
from jax import lax
from jax.experimental import pallas as pl
from jax.experimental.pallas import tpu as pltpu
from jax.sharding import Mesh, PartitionSpec as P


HEAD_SIZE = 128
KEY_VALUE_HEADS = 8
QUERY_HEADS = 16
WIN = 5
GROUP = QUERY_HEADS // KEY_VALUE_HEADS
CORES = 2
KEY_TILE = 256
QUERY_TILE = 128
LANES = 128
PACK = 16
LOG2E = math.log2(math.e)
SCALE = 1.0 / math.sqrt(HEAD_SIZE)
BF16 = jnp.bfloat16
F32 = jnp.float32
CROSS = ("y", "x")
WHOLE = pl.BlockSpec(memory_space=pltpu.VMEM)
SCALARS = pl.BlockSpec(memory_space=pltpu.SMEM)
VMEM_BYTES = 16 * 1024 * 1024


def call(kernel, out_shape, in_specs, flops=0, moved=4 << 20, scratch=()):
    return pl.pallas_call(
        kernel,
        out_shape=out_shape,
        in_specs=in_specs,
        out_specs=jax.tree.map(lambda _: WHOLE, out_shape),
        scratch_shapes=scratch,
        cost_estimate=pl.CostEstimate(flops=flops, bytes_accessed=moved, transcendentals=0),
        compiler_params=pltpu.CompilerParams(vmem_limit_bytes=VMEM_BYTES),
    )


def split3(x):
    hi = x.astype(BF16)
    rest = x - hi.astype(F32)
    mid = rest.astype(BF16)
    low = (rest - mid.astype(F32)).astype(BF16)
    return hi, mid, low


def round_up(n, to):
    return -(-n // to) * to


class Plan:
    def __init__(self, fold, n_x, tokens):
        self.fold, self.n_x, self.tokens = fold, n_x, tokens
        self.chips = fold * n_x
        self.kv_heads = KEY_VALUE_HEADS // self.chips
        self.q_heads = self.kv_heads * GROUP
        self.block = n_x * CORES * tokens
        self.q_rows = self.q_heads * tokens
        self.kv_rows = 2 * self.kv_heads * tokens
        self.aux_sent = round_up(3 * self.q_heads, PACK)
        self.aux = round_up(6 * self.q_heads, PACK)
        self.q_tiles = n_x * tokens // QUERY_TILE
        self.k_tiles = self.block // KEY_TILE
        assert self.k_tiles == 2

    def first_kv_head(self, chip):
        return ((chip % self.n_x) * self.fold + chip // self.n_x) * self.kv_heads


def columns(ref, head):
    return ref.at[:, pl.ds(pl.multiple_of(head * HEAD_SIZE, LANES), HEAD_SIZE)]


def padded_lanes(x):
    rows, width = x.shape
    if width == LANES:
        return x
    return jnp.concatenate([x, jnp.zeros((rows, LANES - width), x.dtype)], axis=1)


def padded_rows(terms, rows):
    have = sum(t.shape[0] for t in terms)
    if have < rows:
        terms = terms + [jnp.zeros((rows - have, LANES), BF16)]
    return jnp.concatenate(terms, axis=0)


def fill_q(plan, me_ref, q_ref, pieces):
    tokens = plan.tokens
    for mask, out in enumerate(pieces):
        kv_head = plan.first_kv_head(me_ref[0] ^ mask)
        for g in range(plan.q_heads):
            out[g * tokens : (g + 1) * tokens, :] = columns(q_ref, kv_head * GROUP + g)[...]


def pack_kernel(plan, me_ref, do_hbm, o_hbm, k_hbm, v_hbm, q_hbm, *refs):
    pieces, q_pieces = refs[: plan.chips], refs[plan.chips : 2 * plan.chips]
    do_ref, o_ref, k_ref, v_ref, q_ref, delta_ref, arrived = refs[2 * plan.chips :]
    tokens = plan.tokens
    half = tokens // 2
    loads = []
    for n, (source, target) in enumerate(
        ((do_hbm, do_ref), (o_hbm, o_ref), (k_hbm, k_ref), (v_hbm, v_ref), (q_hbm, q_ref))
    ):
        pair = []
        for part in range(2):
            rows = pl.ds(part * half, half)
            copy = pltpu.make_async_copy(source.at[rows], target.at[rows], arrived.at[n, part])
            copy.start()
            pair.append(copy)
        loads.append(pair)

    def wait_for(n):
        for copy in loads[n]:
            copy.wait()

    wait_for(0)
    wait_for(1)
    sums = []
    for head in range(QUERY_HEADS):
        cols = slice(head * HEAD_SIZE, (head + 1) * HEAD_SIZE)
        product = do_ref[:, cols].astype(F32) * o_ref[:, cols].astype(F32)
        sums.append(jnp.sum(product, axis=1, keepdims=True))
    sums.append(jnp.zeros((tokens, LANES - QUERY_HEADS), F32))
    delta_ref[...] = padded_lanes(jnp.concatenate(sums, axis=1).T)
    wait_for(2)
    wait_for(3)
    for mask, out in enumerate(pieces):
        kv_head = plan.first_kv_head(me_ref[0] ^ mask)
        terms = []
        for g in range(plan.q_heads):
            head = kv_head * GROUP + g
            out[g * tokens : (g + 1) * tokens, :] = columns(do_ref, head)[...]
            terms.extend(split3(delta_ref[pl.ds(head, 1), :]))
        for h in range(plan.kv_heads):
            at = plan.q_rows + h * tokens
            out[at : at + tokens, :] = columns(k_ref, kv_head + h)[...]
            at += plan.kv_heads * tokens
            out[at : at + tokens, :] = columns(v_ref, kv_head + h)[...]
        out[plan.q_rows + plan.kv_rows :, :] = padded_rows(terms, plan.aux_sent)
    wait_for(4)
    fill_q(plan, me_ref, q_ref, q_pieces)


def pack_q_kernel(plan, me_ref, q_ref, *pieces):
    fill_q(plan, me_ref, q_ref, pieces)


def assemble_kernel(plan, me_ref, lse_ref, *refs):
    pieces, (do_out, kv_out) = refs[:-2], refs[-2:]
    tokens, split = plan.tokens, plan.q_rows + plan.kv_rows
    for mask, piece in enumerate(pieces):
        chip = me_ref[0] ^ mask
        chunk = (chip % plan.n_x) * CORES + me_ref[1]
        do_out[chip, : plan.q_rows, :] = piece[: plan.q_rows, :]
        kv_out[chip] = piece[plan.q_rows : split, :]
        terms = [piece[split : split + 3 * plan.q_heads, :]]
        for g in range(plan.q_heads):
            if tokens == LANES:
                lanes = pl.ds(pl.multiple_of(chunk * LANES, LANES), LANES)
                row = lse_ref[mask // plan.n_x, pl.ds(g, 1), lanes]
            else:
                row = lse_ref[mask // plan.n_x, chunk, pl.ds(g, 1), :]
            terms.extend(split3(row))
        do_out[chip, plan.q_rows :, :] = padded_rows(terms, plan.aux)


def merge_kernel(me_ref, keep_ref, given_ref, *pieces):
    for mask, out in enumerate(pieces):
        chip = me_ref[0] ^ mask
        out[...] = (keep_ref[chip] + given_ref[chip].astype(F32)).astype(BF16)


def lane_row(parts, tokens):
    row = parts[0]
    lane = lax.broadcasted_iota(jnp.int32, row.shape, 1)
    for n, part in enumerate(parts[1:], 1):
        row = jnp.where(lane >= n * tokens, pltpu.roll(part, n * tokens, 1), row)
    return row


def role_kernel(plan, has_dq, me_ref, code_ref, mine_ref, sib_ref, *refs):
    refs = list(refs)
    levels, chips = len(has_dq), plan.chips
    q_pieces = [[refs.pop(0) for _ in range(chips)] for _ in range(levels)]
    do_refs = [refs.pop(0) for _ in range(levels)]
    dq_ins = [refs.pop(0) if has else None for has in has_dq]
    dq_outs = [refs.pop(0) for _ in range(levels)]
    keep, give, kv_ref, q_ref, do_ref, dq_ref, dkv_ref = refs
    core = me_ref[1]
    tokens, n_x, fold = plan.tokens, plan.n_x, plan.fold
    q_per = QUERY_TILE // tokens
    k_per = KEY_TILE // tokens
    kv_ref[core] = mine_ref[...]
    kv_ref[1 - core] = sib_ref[...]
    dkv_ref[...] = jnp.zeros_like(dkv_ref)
    for level in range(levels):
        for mask in range(chips):
            q_ref[level, me_ref[0] ^ mask] = q_pieces[level][mask][...]
        do_ref[level] = do_refs[level][...]
        dq_ref[level] = dq_ins[level][...] if has_dq[level] else jnp.zeros_like(dq_outs[level], F32)

    def q_start(q_in):
        return (q_in * q_per * CORES + core) * tokens

    def q_end(q_in):
        return ((q_in * q_per + q_per - 1) * CORES + core) * tokens + tokens - 1

    last = (((1,), (1,)), ((), ()))

    def row(level, query_block, q_in, key_block, k_tiles, code, masked):
        q_chip = query_block * n_x + q_in * q_per
        tile = query_block * plan.q_tiles + q_in

        def q_part(ref, g):
            return [ref[level, q_chip + n, g * tokens : (g + 1) * tokens, :] for n in range(q_per)]

        def k_place(k_in):
            return [
                (n % CORES, key_block * n_x + k_in * (k_per // CORES) + n // CORES) for n in range(k_per)
            ]

        def k_part(which, h, k_in):
            at = (which * plan.kv_heads + h) * tokens
            return jnp.concatenate([kv_ref[c, chip, at : at + tokens, :] for c, chip in k_place(k_in)], axis=0)

        groups = [do_ref[level, q_chip + n, plan.q_rows :, :].astype(F32) for n in range(q_per)]

        def aux(which, g):
            at = (which * plan.q_heads + g) * 3
            return lane_row([a[at : at + 1] + a[at + 1 : at + 2] + a[at + 2 : at + 3] for a in groups], tokens)

        queries = []
        for h in range(plan.kv_heads):
            heads = range(h * GROUP, (h + 1) * GROUP)
            q2 = jnp.concatenate([r for g in heads for r in q_part(q_ref, g)], axis=0)
            do2 = jnp.concatenate([r for g in heads for r in q_part(do_ref, g)], axis=0)
            delta = jnp.concatenate([aux(0, g) for g in heads], axis=1)
            lse = jnp.concatenate([aux(1, g) for g in heads], axis=1) * LOG2E
            queries.append((q2, do2, delta, lse))
        units = [(h, k_in) for k_in in k_tiles for h in range(plan.kv_heads)]

        def front(unit):
            h, k_in = unit
            q2, do2, _, _ = queries[h]
            k, v = k_part(0, h, k_in), k_part(1, h, k_in)
            scores = lax.dot_general(k, q2, last, preferred_element_type=F32)
            dprobs = lax.dot_general(v, do2, last, preferred_element_type=F32)
            return k, scores, dprobs

        def back(unit, ready):
            h, k_in = unit
            q2, do2, delta, lse = queries[h]
            k, scores, dprobs = ready
            probs = jnp.exp2(scores * (SCALE * LOG2E) - lse)
            if masked:
                key_at = lax.broadcasted_iota(jnp.int32, probs.shape, 0) + k_in * KEY_TILE
                lane = lax.broadcasted_iota(jnp.int32, probs.shape, 1) % QUERY_TILE
                query_at = q_start(q_in) + lane % tokens + (lane // tokens) * (CORES * tokens)
                ahead = key_at - query_at
                allowed = jnp.where(code == 2, ahead, 1 - ahead) <= 0
                probs = jnp.where(allowed, probs, 0.0)
            dscores = (probs * (dprobs - delta) * SCALE).astype(BF16)
            dv = jnp.dot(probs.astype(BF16), do2, preferred_element_type=F32)
            dk = jnp.dot(dscores, q2, preferred_element_type=F32)
            for n, (c, chip) in enumerate(k_place(k_in)):
                rows = slice(n * tokens, (n + 1) * tokens)
                at = h * tokens
                dkv_ref[c, chip, at : at + tokens, :] += dk[rows]
                at += plan.kv_heads * tokens
                dkv_ref[c, chip, at : at + tokens, :] += dv[rows]
            return jnp.dot(k.T, dscores, preferred_element_type=F32)

        ready = front(units[0])
        for n, unit in enumerate(units):
            following = front(units[n + 1]) if n + 1 < len(units) else None
            dq_ref[level, tile, unit[0]] += back(unit, ready)
            ready = following

    def step(index, carry):
        q_in = index % plan.q_tiles
        rest = index // plan.q_tiles
        key_block = rest % fold
        rest = rest // fold
        query_block = rest % fold
        level = rest // fold
        code = code_ref[level, query_block, key_block]
        q_first, q_last = q_start(q_in), q_end(q_in)
        every = tuple(range(plan.k_tiles))
        below = (q_last < (plan.k_tiles - 1) * KEY_TILE) & (code == 2)
        above = (q_first >= KEY_TILE - 1) & (code == 3)

        @pl.when(code == 1)
        def _():
            row(level, query_block, q_in, key_block, every, code, False)

        @pl.when(below | above)
        def _():
            row(level, query_block, q_in, key_block, (jnp.where(below, 0, plan.k_tiles - 1),), code, True)

        @pl.when((code >= 2) & jnp.logical_not(below | above))
        def _():
            row(level, query_block, q_in, key_block, every, code, True)

        return carry

    lax.fori_loop(0, levels * fold * fold * plan.q_tiles, step, 0)
    for level in range(levels):
        dq_outs[level][...] = dq_ref[level].astype(dq_outs[level].dtype)
    keep[...] = dkv_ref[core]
    give[...] = dkv_ref[1 - core].astype(BF16)


def finish_kernel(plan, has_far, me_ref, dq_ref, *refs):
    refs = list(refs)
    far_ref = refs.pop(0) if has_far else None
    pieces, rows_ref = refs[:-1], refs[-1]
    tokens = plan.tokens
    q_per = QUERY_TILE // tokens
    for tile in range(dq_ref.shape[0]):
        for h in range(plan.kv_heads):
            total = dq_ref[tile, h]
            if has_far:
                total = total + far_ref[tile, h].astype(F32)
            turned = total.T.astype(BF16)
            for g in range(GROUP):
                for n in range(q_per):
                    at = (h * GROUP + g) * tokens
                    source = g * QUERY_TILE + n * tokens
                    rows_ref[tile * q_per + n, at : at + tokens, :] = turned[source : source + tokens]
    for mask, out in enumerate(pieces):
        out[...] = rows_ref[me_ref[0] ^ mask]


def unpack_kernel(plan, levels, me_ref, *refs):
    refs = list(refs)
    dq_pieces = [refs.pop(0) for _ in range(plan.chips)]
    kv_pieces = [[refs.pop(0) for _ in range(plan.chips)] for _ in range(levels)]
    dq_ref, dk_ref, dv_ref = refs
    tokens = plan.tokens
    for mask in range(plan.chips):
        kv_head = plan.first_kv_head(me_ref[0] ^ mask)
        for g in range(plan.q_heads):
            columns(dq_ref, kv_head * GROUP + g)[...] = dq_pieces[mask][g * tokens : (g + 1) * tokens, :]
        total = kv_pieces[0][mask][...]
        if levels > 1:
            total = total.astype(F32)
            for level in range(1, levels):
                total = total + kv_pieces[level][mask][...].astype(F32)
            total = total.astype(BF16)
        for h in range(plan.kv_heads):
            columns(dk_ref, kv_head + h)[...] = total[h * tokens : (h + 1) * tokens]
            at = (plan.kv_heads + h) * tokens
            columns(dv_ref, kv_head + h)[...] = total[at : at + tokens]


def exchange(pieces):
    chips = len(pieces)
    return [pieces[0]] + [
        lax.ppermute(pieces[mask], CROSS, [(i, i ^ mask) for i in range(chips)])
        for mask in range(1, chips)
    ]


def deliver(pieces, planes, level):
    chips = len(pieces)
    return [
        lax.ppermute(
            pieces[mask],
            ("z",) + CROSS,
            [(p * chips + i, (p - level) * chips + (i ^ mask)) for p in range(level, planes) for i in range(chips)],
        )
        for mask in range(chips)
    ]


def swap(value):
    return lax.ppermute(value, "core", [(0, 1), (1, 0)])


def along(value, planes, steps):
    pairs = [(i, i + steps) for i in range(planes) if 0 <= i + steps < planes]
    return lax.ppermute(value, "z", pairs)


def query_levels(level, reach):
    return [d - level for d in (2 * level - 1, 2 * level) if 0 <= d <= reach]


def plane_logsum(logsum, plan, y, core):
    other = swap(logsum)
    both = jnp.where(core == 0, jnp.concatenate([logsum, other]), jnp.concatenate([other, logsum]))
    rows = both.reshape(plan.fold, plan.q_heads, plan.block)
    parts = []
    for mask in range(plan.fold):
        part = lax.dynamic_index_in_dim(rows, y ^ mask, 0, keepdims=False)
        if mask:
            part = lax.ppermute(part, "y", [(i, i ^ mask) for i in range(plan.fold)])
        parts.append(part)
    lse = jnp.stack(parts)
    if plan.tokens == LANES:
        return lse
    lse = lse.reshape(plan.fold, plan.q_heads, plan.n_x * CORES, plan.tokens).transpose(0, 2, 1, 3)
    return jnp.pad(lse, ((0, 0), (0, 0), (0, 0), (0, LANES - plan.tokens)))


def body(queries, output_gradient, outputs, key_vectors, values, logsum, pair_list):
    planes, fold, n_x = (lax.axis_size(a) for a in ("z", "y", "x"))
    plan = Plan(fold, n_x, queries.shape[0])
    chips = plan.chips
    reach = -(-(WIN - 1) // fold)
    z, y, x, core = (lax.axis_index(a) for a in ("z", "y", "x", "core"))
    me = jnp.stack([y * n_x + x, core]).astype(jnp.int32)

    def like(rows):
        return jax.ShapeDtypeStruct((rows, LANES), BF16)

    def stacked(rows, dtype=BF16):
        return jax.ShapeDtypeStruct((chips, rows, LANES), dtype)

    raw = [queries]
    for _ in range(1, reach // 2 + 1):
        raw.append(along(raw[-1], planes, -1))

    lse = plane_logsum(logsum, plan, y, core)
    arrays = (output_gradient, outputs, key_vectors, values, queries)
    packed = call(
        functools.partial(pack_kernel, plan),
        [like(plan.q_rows + plan.kv_rows + plan.aux_sent)] * chips + [like(plan.q_rows)] * chips,
        [SCALARS] + [pl.BlockSpec(memory_space=pltpu.HBM)] * len(arrays),
        scratch=[pltpu.VMEM(a.shape, a.dtype) for a in arrays]
        + [pltpu.VMEM((LANES, LANES), F32), pltpu.SemaphoreType.DMA((len(arrays), 2))],
    )(me, *arrays)
    pieces, q_pieces = packed[:chips], packed[chips:]
    do_own, kv_own = call(
        functools.partial(assemble_kernel, plan),
        [stacked(plan.q_rows + plan.aux), stacked(plan.kv_rows)],
        [SCALARS] + [WHOLE] * (chips + 1),
    )(me, lse, *exchange(pieces))

    up = [kv_own]
    for _ in range(1, (reach + 1) // 2 + 1):
        up.append(along(up[-1], planes, 1))
    far_do = [do_own]
    for _ in range(1, reach // 2 + 1):
        far_do.append(along(far_do[-1], planes, -1))
    all_q = [exchange(q_pieces)]
    for n in range(1, len(raw)):
        far_pieces = call(
            functools.partial(pack_q_kernel, plan), [like(plan.q_rows)] * chips, [SCALARS, WHOLE]
        )(me, raw[n])
        all_q.append(exchange(far_pieces))
    up = [(kv, swap(kv)) for kv in up]

    grad_q = [None] * len(all_q)
    grad_kv = []
    dq_shape = (fold * plan.q_tiles, plan.kv_heads, HEAD_SIZE, GROUP * QUERY_TILE)
    inside = jnp.arange(fold, dtype=jnp.int32)
    for i, (mine, sibling) in enumerate(up):
        levels = query_levels(i, reach)
        query_blocks = (z + jnp.array(levels, jnp.int32)[:, None]) * fold + inside
        key_blocks = (z - i) * fold + inside
        row = pair_list[:, :, None, None, None]
        hit = (row[:, 0] == query_blocks[:, :, None]) & (row[:, 1] == key_blocks)
        codes = jnp.sum(jnp.where(hit, row[:, 2] + 1, 0), axis=0).astype(jnp.int32)
        has_dq = tuple(grad_q[j] is not None for j in levels)
        over = [j and j not in query_levels(i + 1, reach) for j in levels]
        *parts, keep, give = call(
            functools.partial(role_kernel, plan, has_dq),
            [jax.ShapeDtypeStruct(dq_shape, BF16 if done else F32) for done in over]
            + [stacked(plan.kv_rows, F32), stacked(plan.kv_rows)],
            [SCALARS] * 2 + [WHOLE] * (2 + len(levels) * (chips + 1) + sum(has_dq)),
            flops=10 * len(levels) * fold * fold * plan.q_heads * plan.block * plan.block * HEAD_SIZE // CORES,
            scratch=[
                pltpu.VMEM((CORES, chips, plan.kv_rows, LANES), BF16),
                pltpu.VMEM((len(levels), chips, plan.q_rows, LANES), BF16),
                pltpu.VMEM((len(levels), chips, plan.q_rows + plan.aux, LANES), BF16),
                pltpu.VMEM((len(levels),) + dq_shape, F32),
                pltpu.VMEM((CORES, chips, plan.kv_rows, LANES), F32),
            ],
        )(
            me,
            codes,
            mine,
            sibling,
            *[piece for j in levels for piece in all_q[j]],
            *[far_do[j] for j in levels],
            *[grad_q[j] for j in levels if grad_q[j] is not None],
        )
        for j, part in zip(levels, parts):
            grad_q[j] = part
        merged = call(merge_kernel, [like(plan.kv_rows)] * chips, [SCALARS] + [WHOLE] * 2)(me, keep, swap(give))
        grad_kv.append(deliver(merged, planes, i) if i else exchange(merged))

    far_q = None
    for level in range(len(grad_q) - 1, 0, -1):
        part = grad_q[level]
        if far_q is not None:
            part = (part.astype(F32) + far_q.astype(F32)).astype(BF16)
        far_q = along(part, planes, 1)
    dq_pieces = call(
        functools.partial(finish_kernel, plan, far_q is not None),
        [like(plan.q_rows)] * chips,
        [SCALARS, WHOLE] + [WHOLE] * (far_q is not None),
        scratch=[pltpu.VMEM((chips, plan.q_rows, LANES), BF16)],
    )(me, grad_q[0], *([] if far_q is None else [far_q]))
    return tuple(
        call(
            functools.partial(unpack_kernel, plan, len(grad_kv)),
            [
                jax.ShapeDtypeStruct((plan.tokens, QUERY_HEADS * HEAD_SIZE), BF16),
                jax.ShapeDtypeStruct((plan.tokens, KEY_VALUE_HEADS * HEAD_SIZE), BF16),
                jax.ShapeDtypeStruct((plan.tokens, KEY_VALUE_HEADS * HEAD_SIZE), BF16),
            ],
            [SCALARS] + [WHOLE] * (chips * (1 + len(grad_kv))),
        )(me, *exchange(dq_pieces), *[piece for level in grad_kv for piece in level])
    )


def solution(mesh):
    n_seq, n_head = mesh.shape["seq"], mesh.shape["head"]
    fold = KEY_VALUE_HEADS // n_head
    assert n_head * fold == KEY_VALUE_HEADS and n_seq % fold == 0 and n_head % CORES == 0
    names = ("z", "y", "x", "core")
    planes = Mesh(mesh.devices.reshape(n_seq // fold, fold, n_head // CORES, CORES), names)
    rows = P(names, None)
    return jax.shard_map(
        body,
        mesh=planes,
        in_specs=(rows,) * 5 + (P(("x", "core"), ("z", "y")), P()),
        out_specs=(rows,) * 3,
        check_vma=False,
    )
```

```python
import functools
import math

import jax
import jax.numpy as jnp
from jax import lax
from jax.experimental import pallas as pl
from jax.experimental.pallas import tpu as pltpu
from jax.sharding import Mesh, PartitionSpec as P


HEAD_SIZE = 128
KEY_VALUE_HEADS = 8
QUERY_HEADS = 16
WIN = 5
GROUP = QUERY_HEADS // KEY_VALUE_HEADS
CORES = 2
KEY_TILE = 256
QUERY_TILE = 128
LANES = 128
PACK = 16
LOG2E = math.log2(math.e)
SCALE = 1.0 / math.sqrt(HEAD_SIZE)
BF16 = jnp.bfloat16
F32 = jnp.float32
CROSS = ("y", "x")
WHOLE = pl.BlockSpec(memory_space=pltpu.VMEM)
SCALARS = pl.BlockSpec(memory_space=pltpu.SMEM)
VMEM_BYTES = 16 * 1024 * 1024


def call(kernel, out_shape, in_specs, flops=0, moved=4 << 20, scratch=(), vmem=VMEM_BYTES):
    def placed(*refs):
        n_x = lax.axis_size("x")
        return kernel((lax.axis_index("y") * n_x + lax.axis_index("x"), lax.axis_index("core")), *refs)

    return pl.pallas_call(
        placed,
        out_shape=out_shape,
        in_specs=in_specs,
        out_specs=jax.tree.map(lambda _: WHOLE, out_shape),
        scratch_shapes=scratch,
        cost_estimate=pl.CostEstimate(flops=flops, bytes_accessed=moved, transcendentals=0),
        compiler_params=pltpu.CompilerParams(vmem_limit_bytes=vmem),
    )


def split3(x):
    hi = x.astype(BF16)
    rest = x - hi.astype(F32)
    mid = rest.astype(BF16)
    low = (rest - mid.astype(F32)).astype(BF16)
    return hi, mid, low


def round_up(n, to):
    return -(-n // to) * to


class Plan:
    def __init__(self, fold, n_x, tokens):
        self.fold, self.n_x, self.tokens = fold, n_x, tokens
        self.chips = fold * n_x
        self.kv_heads = KEY_VALUE_HEADS // self.chips
        self.q_heads = self.kv_heads * GROUP
        self.block = n_x * CORES * tokens
        self.q_rows = self.q_heads * tokens
        self.kv_rows = 2 * self.kv_heads * tokens
        self.aux_sent = round_up(3 * self.q_heads, PACK)
        self.aux = round_up(6 * self.q_heads, PACK)
        self.q_tiles = n_x * tokens // QUERY_TILE
        self.k_tiles = self.block // KEY_TILE
        assert self.k_tiles == 2

    def first_kv_head(self, chip):
        return ((chip % self.n_x) * self.fold + chip // self.n_x) * self.kv_heads


def columns(ref, head):
    return ref.at[:, pl.ds(pl.multiple_of(head * HEAD_SIZE, LANES), HEAD_SIZE)]


def padded_lanes(x):
    rows, width = x.shape
    if width == LANES:
        return x
    return jnp.concatenate([x, jnp.zeros((rows, LANES - width), x.dtype)], axis=1)


def padded_rows(terms, rows):
    have = sum(t.shape[0] for t in terms)
    if have < rows:
        terms = terms + [jnp.zeros((rows - have, LANES), BF16)]
    return jnp.concatenate(terms, axis=0)


def pack_kernel(plan, me, do_hbm, o_hbm, k_hbm, v_hbm, *refs):
    pieces, (do_ref, o_ref, k_ref, v_ref, delta_ref, arrived) = refs[: plan.chips], refs[plan.chips :]
    tokens = plan.tokens
    half = tokens // 2
    loads = []
    for n, (source, target) in enumerate(
        ((do_hbm, do_ref), (o_hbm, o_ref), (k_hbm, k_ref), (v_hbm, v_ref))
    ):
        pair = []
        for part in range(2):
            rows = pl.ds(part * half, half)
            copy = pltpu.make_async_copy(source.at[rows], target.at[rows], arrived.at[n, part])
            copy.start()
            pair.append(copy)
        loads.append(pair)

    def wait_for(n):
        for copy in loads[n]:
            copy.wait()

    wait_for(0)
    wait_for(1)
    sums = []
    for head in range(QUERY_HEADS):
        cols = slice(head * HEAD_SIZE, (head + 1) * HEAD_SIZE)
        product = do_ref[:, cols].astype(F32) * o_ref[:, cols].astype(F32)
        sums.append(jnp.sum(product, axis=1, keepdims=True))
    sums.append(jnp.zeros((tokens, LANES - QUERY_HEADS), F32))
    delta_ref[...] = padded_lanes(jnp.concatenate(sums, axis=1).T)
    wait_for(2)
    wait_for(3)
    for mask, out in enumerate(pieces):
        kv_head = plan.first_kv_head(me[0] ^ mask)
        terms = []
        for g in range(plan.q_heads):
            head = kv_head * GROUP + g
            out[g * tokens : (g + 1) * tokens, :] = columns(do_ref, head)[...]
            terms.extend(split3(delta_ref[pl.ds(head, 1), :]))
        for h in range(plan.kv_heads):
            at = plan.q_rows + h * tokens
            out[at : at + tokens, :] = columns(k_ref, kv_head + h)[...]
            at += plan.kv_heads * tokens
            out[at : at + tokens, :] = columns(v_ref, kv_head + h)[...]
        out[plan.q_rows + plan.kv_rows :, :] = padded_rows(terms, plan.aux_sent)


def pack_q_kernel(plan, me, *refs):
    levels, pieces = refs[: -plan.chips], refs[-plan.chips :]
    tokens = plan.tokens
    for mask, out in enumerate(pieces):
        first = plan.first_kv_head(me[0] ^ mask) * GROUP
        for level, ref in enumerate(levels):
            for g in range(plan.q_heads):
                at = level * plan.q_rows + g * tokens
                out[at : at + tokens, :] = columns(ref, first + g)[...]


def ordered_kernel(me, *refs):
    pieces, out = refs[:-1], refs[-1]
    for mask, piece in enumerate(pieces):
        out[me[0] ^ mask] = piece[...]


def assemble_kernel(plan, me, lse_ref, *refs):
    pieces, (do_out, kv_out) = refs[:-2], refs[-2:]
    tokens, split = plan.tokens, plan.q_rows + plan.kv_rows
    for mask, piece in enumerate(pieces):
        chip = me[0] ^ mask
        chunk = (chip % plan.n_x) * CORES + me[1]
        do_out[chip, : plan.q_rows, :] = piece[: plan.q_rows, :]
        kv_out[chip] = piece[plan.q_rows : split, :]
        terms = [piece[split : split + 3 * plan.q_heads, :]]
        for g in range(plan.q_heads):
            if tokens == LANES:
                lanes = pl.ds(pl.multiple_of(chunk * LANES, LANES), LANES)
                row = lse_ref[mask // plan.n_x, pl.ds(g, 1), lanes]
            else:
                row = lse_ref[mask // plan.n_x, chunk, pl.ds(g, 1), :]
            terms.extend(split3(row))
        do_out[chip, plan.q_rows :, :] = padded_rows(terms, plan.aux)


def merge_kernel(me, keep_ref, given_ref, *pieces):
    for mask, out in enumerate(pieces):
        chip = me[0] ^ mask
        out[...] = (keep_ref[chip] + given_ref[chip].astype(F32)).astype(BF16)


def lane_row(parts, tokens):
    row = parts[0]
    lane = lax.broadcasted_iota(jnp.int32, row.shape, 1)
    for n, part in enumerate(parts[1:], 1):
        row = jnp.where(lane >= n * tokens, pltpu.roll(part, n * tokens, 1), row)
    return row


def role_kernel(plan, at_level, has_dq, me, code_ref, mine_ref, sib_ref, *refs):
    refs = list(refs)
    levels, chips = len(has_dq), plan.chips
    q_pieces = [refs.pop(0) for _ in range(chips)]
    do_refs = [refs.pop(0) for _ in range(levels)]
    dq_ins = [refs.pop(0) if has else None for has in has_dq]
    dq_outs = [refs.pop(0) for _ in range(levels)]
    keep, give, kv_ref, q_ref, do_ref, dq_ref, dkv_ref = refs
    core = me[1]
    tokens, n_x, fold = plan.tokens, plan.n_x, plan.fold
    q_per = QUERY_TILE // tokens
    k_per = KEY_TILE // tokens
    kv_ref[core] = mine_ref[...]
    kv_ref[1 - core] = sib_ref[...]
    dkv_ref[...] = jnp.zeros_like(dkv_ref)
    for level in range(levels):
        for mask in range(chips):
            first = at_level[level] * plan.q_rows
            q_ref[level, me[0] ^ mask] = q_pieces[mask][first : first + plan.q_rows, :]
        do_ref[level] = do_refs[level][...]
        dq_ref[level] = dq_ins[level][...] if has_dq[level] else jnp.zeros_like(dq_outs[level], F32)

    def q_start(q_in):
        return (q_in * q_per * CORES + core) * tokens

    def q_end(q_in):
        return ((q_in * q_per + q_per - 1) * CORES + core) * tokens + tokens - 1

    last = (((1,), (1,)), ((), ()))

    def row(level, query_block, q_in, key_block, k_tiles, code, masked):
        q_chip = query_block * n_x + q_in * q_per
        tile = query_block * plan.q_tiles + q_in

        def q_part(ref, g):
            return [ref[level, q_chip + n, g * tokens : (g + 1) * tokens, :] for n in range(q_per)]

        def k_place(k_in):
            return [
                (n % CORES, key_block * n_x + k_in * (k_per // CORES) + n // CORES) for n in range(k_per)
            ]

        def k_part(which, h, k_in):
            at = (which * plan.kv_heads + h) * tokens
            return jnp.concatenate([kv_ref[c, chip, at : at + tokens, :] for c, chip in k_place(k_in)], axis=0)

        groups = [do_ref[level, q_chip + n, plan.q_rows :, :].astype(F32) for n in range(q_per)]

        def aux(which, g):
            at = (which * plan.q_heads + g) * 3
            return lane_row([a[at : at + 1] + a[at + 1 : at + 2] + a[at + 2 : at + 3] for a in groups], tokens)

        queries = []
        for h in range(plan.kv_heads):
            heads = range(h * GROUP, (h + 1) * GROUP)
            q2 = jnp.concatenate([r for g in heads for r in q_part(q_ref, g)], axis=0)
            do2 = jnp.concatenate([r for g in heads for r in q_part(do_ref, g)], axis=0)
            delta = jnp.concatenate([aux(0, g) for g in heads], axis=1)
            lse = jnp.concatenate([aux(1, g) for g in heads], axis=1) * LOG2E
            queries.append((q2, do2, delta, lse))
        units = [(h, k_in) for k_in in k_tiles for h in range(plan.kv_heads)]

        def front(unit):
            h, k_in = unit
            q2, do2, _, _ = queries[h]
            k, v = k_part(0, h, k_in), k_part(1, h, k_in)
            scores = lax.dot_general(k, q2, last, preferred_element_type=F32)
            dprobs = lax.dot_general(v, do2, last, preferred_element_type=F32)
            return k, scores, dprobs

        def back(unit, ready):
            h, k_in = unit
            q2, do2, delta, lse = queries[h]
            k, scores, dprobs = ready
            probs = jnp.exp2(scores * (SCALE * LOG2E) - lse)
            if masked:
                key_at = lax.broadcasted_iota(jnp.int32, probs.shape, 0) + k_in * KEY_TILE
                lane = lax.broadcasted_iota(jnp.int32, probs.shape, 1) % QUERY_TILE
                query_at = q_start(q_in) + lane % tokens + (lane // tokens) * (CORES * tokens)
                ahead = key_at - query_at
                allowed = jnp.where(code == 2, ahead, 1 - ahead) <= 0
                probs = jnp.where(allowed, probs, 0.0)
            dscores = (probs * (dprobs - delta) * SCALE).astype(BF16)
            dv = jnp.dot(probs.astype(BF16), do2, preferred_element_type=F32)
            dk = jnp.dot(dscores, q2, preferred_element_type=F32)
            for n, (c, chip) in enumerate(k_place(k_in)):
                rows = slice(n * tokens, (n + 1) * tokens)
                at = h * tokens
                dkv_ref[c, chip, at : at + tokens, :] += dk[rows]
                at += plan.kv_heads * tokens
                dkv_ref[c, chip, at : at + tokens, :] += dv[rows]
            return jnp.dot(k.T, dscores, preferred_element_type=F32)

        ready = front(units[0])
        for n, unit in enumerate(units):
            following = front(units[n + 1]) if n + 1 < len(units) else None
            dq_ref[level, tile, unit[0]] += back(unit, ready)
            ready = following

    def step(index, carry):
        q_in = index % plan.q_tiles
        rest = index // plan.q_tiles
        key_block = rest % fold
        rest = rest // fold
        query_block = rest % fold
        level = rest // fold
        code = code_ref[level, query_block, key_block]
        q_first, q_last = q_start(q_in), q_end(q_in)
        every = tuple(range(plan.k_tiles))
        below = (q_last < (plan.k_tiles - 1) * KEY_TILE) & (code == 2)
        above = (q_first >= KEY_TILE - 1) & (code == 3)

        @pl.when(code == 1)
        def _():
            row(level, query_block, q_in, key_block, every, code, False)

        @pl.when(below | above)
        def _():
            row(level, query_block, q_in, key_block, (jnp.where(below, 0, plan.k_tiles - 1),), code, True)

        @pl.when((code >= 2) & jnp.logical_not(below | above))
        def _():
            row(level, query_block, q_in, key_block, every, code, True)

        return carry

    lax.fori_loop(0, levels * fold * fold * plan.q_tiles, step, 0)
    for level in range(levels):
        dq_outs[level][...] = dq_ref[level].astype(dq_outs[level].dtype)
    keep[...] = dkv_ref[core]
    give[...] = dkv_ref[1 - core].astype(BF16)


def finish_kernel(plan, has_far, me, dq_ref, *refs):
    refs = list(refs)
    far_ref = refs.pop(0) if has_far else None
    pieces, rows_ref = refs[:-1], refs[-1]
    tokens = plan.tokens
    q_per = QUERY_TILE // tokens
    for tile in range(dq_ref.shape[0]):
        for h in range(plan.kv_heads):
            total = dq_ref[tile, h]
            if has_far:
                total = total + far_ref[tile, h].astype(F32)
            turned = total.T.astype(BF16)
            for g in range(GROUP):
                for n in range(q_per):
                    at = (h * GROUP + g) * tokens
                    source = g * QUERY_TILE + n * tokens
                    rows_ref[tile * q_per + n, at : at + tokens, :] = turned[source : source + tokens]
    for mask, out in enumerate(pieces):
        out[...] = rows_ref[me[0] ^ mask]


def unpack_kernel(plan, has_far, me, *refs):
    refs = list(refs)
    dq_pieces = [refs.pop(0) for _ in range(plan.chips)]
    kv_pieces = [refs.pop(0) for _ in range(plan.chips)]
    far_ref = refs.pop(0) if has_far else None
    dq_ref, dk_ref, dv_ref = refs
    tokens = plan.tokens
    for mask in range(plan.chips):
        chip = me[0] ^ mask
        kv_head = plan.first_kv_head(chip)
        for g in range(plan.q_heads):
            columns(dq_ref, kv_head * GROUP + g)[...] = dq_pieces[mask][g * tokens : (g + 1) * tokens, :]
        total = kv_pieces[mask][...]
        if has_far:
            total = (total.astype(F32) + far_ref[chip].astype(F32)).astype(BF16)
        for h in range(plan.kv_heads):
            columns(dk_ref, kv_head + h)[...] = total[h * tokens : (h + 1) * tokens]
            at = (plan.kv_heads + h) * tokens
            columns(dv_ref, kv_head + h)[...] = total[at : at + tokens]


def exchange(pieces):
    chips = len(pieces)
    return [pieces[0]] + [
        lax.ppermute(pieces[mask], CROSS, [(i, i ^ mask) for i in range(chips)])
        for mask in range(1, chips)
    ]


def swap(value):
    return lax.ppermute(value, "core", [(0, 1), (1, 0)])


def along(value, planes, steps):
    pairs = [(i, i + steps) for i in range(planes) if 0 <= i + steps < planes]
    return lax.ppermute(value, "z", pairs)


def query_levels(level, reach):
    return [d - level for d in (2 * level - 1, 2 * level) if 0 <= d <= reach]


def plane_logsum(logsum, plan, y, core):
    blocks = [logsum]
    for mask in range(1, plan.fold):
        blocks.append(lax.ppermute(logsum, "y", [(i, i ^ mask) for i in range(plan.fold)]))
    mine = jnp.stack(blocks)
    other = swap(mine)
    both = jnp.where(core == 0, jnp.concatenate([mine, other], axis=1), jnp.concatenate([other, mine], axis=1))
    lse = lax.dynamic_slice_in_dim(both, y * plan.q_heads, plan.q_heads, axis=1)
    if plan.tokens == LANES:
        return lse
    lse = lse.reshape(plan.fold, plan.q_heads, plan.n_x * CORES, plan.tokens).transpose(0, 2, 1, 3)
    return jnp.pad(lse, ((0, 0), (0, 0), (0, 0), (0, LANES - plan.tokens)))


def body(queries, output_gradient, outputs, key_vectors, values, logsum, pair_list):
    planes, fold, n_x = (lax.axis_size(a) for a in ("z", "y", "x"))
    plan = Plan(fold, n_x, queries.shape[0])
    chips = plan.chips
    reach = -(-(WIN - 1) // fold)
    z, y, core = (lax.axis_index(a) for a in ("z", "y", "core"))

    def like(rows):
        return jax.ShapeDtypeStruct((rows, LANES), BF16)

    def stacked(rows, dtype=BF16):
        return jax.ShapeDtypeStruct((chips, rows, LANES), dtype)

    raw = [queries]
    for _ in range(1, reach // 2 + 1):
        raw.append(along(raw[-1], planes, -1))

    lse = plane_logsum(logsum, plan, y, core)
    arrays = (output_gradient, outputs, key_vectors, values)
    pieces = call(
        functools.partial(pack_kernel, plan),
        [like(plan.q_rows + plan.kv_rows + plan.aux_sent)] * chips,
        [pl.BlockSpec(memory_space=pltpu.HBM)] * len(arrays),
        scratch=[pltpu.VMEM(a.shape, a.dtype) for a in arrays]
        + [pltpu.VMEM((LANES, LANES), F32), pltpu.SemaphoreType.DMA((len(arrays), 2))],
        vmem=60 * 1024 * 1024,
    )(*arrays)
    do_own, kv_own = call(
        functools.partial(assemble_kernel, plan),
        [stacked(plan.q_rows + plan.aux), stacked(plan.kv_rows)],
        [WHOLE] * (chips + 1),
    )(lse, *exchange(pieces))

    up = [kv_own]
    for _ in range(1, (reach + 1) // 2 + 1):
        up.append(along(up[-1], planes, 1))
    far_do = [do_own]
    for _ in range(1, reach // 2 + 1):
        far_do.append(along(far_do[-1], planes, -1))
    q_pieces = exchange(
        call(functools.partial(pack_q_kernel, plan), [like(len(raw) * plan.q_rows)] * chips, [WHOLE] * len(raw))(*raw),
    )
    up = [(kv, swap(kv)) for kv in up]

    grad_q = [None] * len(raw)
    grad_kv = []
    dq_shape = (fold * plan.q_tiles, plan.kv_heads, HEAD_SIZE, GROUP * QUERY_TILE)
    inside = jnp.arange(fold, dtype=jnp.int32)
    for i, (mine, sibling) in enumerate(up):
        levels = query_levels(i, reach)
        query_blocks = (z + jnp.array(levels, jnp.int32)[:, None]) * fold + inside
        key_blocks = (z - i) * fold + inside
        row = pair_list[:, :, None, None, None]
        hit = (row[:, 0] == query_blocks[:, :, None]) & (row[:, 1] == key_blocks)
        codes = jnp.sum(jnp.where(hit, row[:, 2] + 1, 0), axis=0).astype(jnp.int32)
        has_dq = tuple(grad_q[j] is not None for j in levels)
        over = [j and j not in query_levels(i + 1, reach) for j in levels]
        *parts, keep, give = call(
            functools.partial(role_kernel, plan, tuple(levels), has_dq),
            [jax.ShapeDtypeStruct(dq_shape, BF16 if done else F32) for done in over]
            + [stacked(plan.kv_rows, F32), stacked(plan.kv_rows)],
            [SCALARS] + [WHOLE] * (2 + chips + len(levels) + sum(has_dq)),
            flops=10 * len(levels) * fold * fold * plan.q_heads * plan.block * plan.block * HEAD_SIZE // CORES,
            scratch=[
                pltpu.VMEM((CORES, chips, plan.kv_rows, LANES), BF16),
                pltpu.VMEM((len(levels), chips, plan.q_rows, LANES), BF16),
                pltpu.VMEM((len(levels), chips, plan.q_rows + plan.aux, LANES), BF16),
                pltpu.VMEM((len(levels),) + dq_shape, F32),
                pltpu.VMEM((CORES, chips, plan.kv_rows, LANES), F32),
            ],
        )(
            codes,
            mine,
            sibling,
            *q_pieces,
            *[far_do[j] for j in levels],
            *[grad_q[j] for j in levels if grad_q[j] is not None],
        )
        for j, part in zip(levels, parts):
            grad_q[j] = part
        merged = call(merge_kernel, [like(plan.kv_rows)] * chips, [WHOLE] * 2)(keep, swap(give))
        grad_kv.append(exchange(merged))

    def plus(part, far):
        return part if far is None else (part.astype(F32) + far.astype(F32)).astype(BF16)

    far_kv = None
    for level in range(len(grad_kv) - 1, 0, -1):
        part = call(ordered_kernel, stacked(plan.kv_rows), [WHOLE] * chips)(*grad_kv[level])
        far_kv = along(plus(part, far_kv), planes, -1)
    far_q = None
    for level in range(len(grad_q) - 1, 0, -1):
        far_q = along(plus(grad_q[level], far_q), planes, 1)
    dq_pieces = call(
        functools.partial(finish_kernel, plan, far_q is not None),
        [like(plan.q_rows)] * chips,
        [WHOLE] + [WHOLE] * (far_q is not None),
        scratch=[pltpu.VMEM((chips, plan.q_rows, LANES), BF16)],
    )(grad_q[0], *([] if far_q is None else [far_q]))
    return tuple(
        call(
            functools.partial(unpack_kernel, plan, far_kv is not None),
            [
                jax.ShapeDtypeStruct((plan.tokens, QUERY_HEADS * HEAD_SIZE), BF16),
                jax.ShapeDtypeStruct((plan.tokens, KEY_VALUE_HEADS * HEAD_SIZE), BF16),
                jax.ShapeDtypeStruct((plan.tokens, KEY_VALUE_HEADS * HEAD_SIZE), BF16),
            ],
            [WHOLE] * (2 * chips + (far_kv is not None)),
        )(*exchange(dq_pieces), *grad_kv[0], *([] if far_kv is None else [far_kv]))
    )


def solution(mesh):
    n_seq, n_head = mesh.shape["seq"], mesh.shape["head"]
    fold = KEY_VALUE_HEADS // n_head
    assert n_head * fold == KEY_VALUE_HEADS and n_seq % fold == 0 and n_head % CORES == 0
    names = ("z", "y", "x", "core")
    planes = Mesh(mesh.devices.reshape(n_seq // fold, fold, n_head // CORES, CORES), names)
    rows = P(names, None)
    return jax.shard_map(
        body,
        mesh=planes,
        in_specs=(rows,) * 5 + (P(("x", "core"), ("z", "y")), P()),
        out_specs=(rows,) * 3,
        check_vma=False,
    )
```

```python
import functools
import math

import jax
import jax.numpy as jnp
from jax import lax
from jax.experimental import pallas as pl
from jax.experimental.pallas import tpu as pltpu
from jax.sharding import Mesh, PartitionSpec as P


HEAD_SIZE = 128
KEY_VALUE_HEADS = 8
QUERY_HEADS = 16
WIN = 5
GROUP = QUERY_HEADS // KEY_VALUE_HEADS
CORES = 2
KEY_TILE = 256
QUERY_TILE = 128
LANES = 128
PACK = 16
LOG2E = math.log2(math.e)
SCALE = 1.0 / math.sqrt(HEAD_SIZE)
BF16 = jnp.bfloat16
F32 = jnp.float32
CROSS = ("y", "x")
WHOLE = pl.BlockSpec(memory_space=pltpu.VMEM)
SCALARS = pl.BlockSpec(memory_space=pltpu.SMEM)
VMEM_BYTES = 16 * 1024 * 1024


def call(kernel, out_shape, in_specs, flops=0, moved=4 << 20, scratch=(), vmem=VMEM_BYTES):
    def placed(*refs):
        n_x = lax.axis_size("x")
        return kernel((lax.axis_index("y") * n_x + lax.axis_index("x"), lax.axis_index("core")), *refs)

    return pl.pallas_call(
        placed,
        out_shape=out_shape,
        in_specs=in_specs,
        out_specs=jax.tree.map(lambda _: WHOLE, out_shape),
        scratch_shapes=scratch,
        cost_estimate=pl.CostEstimate(flops=flops, bytes_accessed=moved, transcendentals=0),
        compiler_params=pltpu.CompilerParams(vmem_limit_bytes=vmem),
    )


def split3(x):
    hi = x.astype(BF16)
    rest = x - hi.astype(F32)
    mid = rest.astype(BF16)
    low = (rest - mid.astype(F32)).astype(BF16)
    return hi, mid, low


def round_up(n, to):
    return -(-n // to) * to


class Plan:
    def __init__(self, fold, n_x, tokens):
        self.fold, self.n_x, self.tokens = fold, n_x, tokens
        self.chips = fold * n_x
        self.kv_heads = KEY_VALUE_HEADS // self.chips
        self.q_heads = self.kv_heads * GROUP
        self.block = n_x * CORES * tokens
        self.q_rows = self.q_heads * tokens
        self.kv_rows = 2 * self.kv_heads * tokens
        self.aux_sent = round_up(3 * self.q_heads, PACK)
        self.aux = round_up(6 * self.q_heads, PACK)
        self.q_tiles = n_x * tokens // QUERY_TILE
        self.k_tiles = self.block // KEY_TILE
        assert self.k_tiles == 2

    def first_kv_head(self, chip):
        return ((chip % self.n_x) * self.fold + chip // self.n_x) * self.kv_heads


def columns(ref, head):
    return ref.at[:, pl.ds(pl.multiple_of(head * HEAD_SIZE, LANES), HEAD_SIZE)]


def padded_lanes(x):
    rows, width = x.shape
    if width == LANES:
        return x
    return jnp.concatenate([x, jnp.zeros((rows, LANES - width), x.dtype)], axis=1)


def padded_rows(terms, rows):
    have = sum(t.shape[0] for t in terms)
    if have < rows:
        terms = terms + [jnp.zeros((rows - have, LANES), BF16)]
    return jnp.concatenate(terms, axis=0)


def pack_kernel(plan, me, do_hbm, o_hbm, k_hbm, v_hbm, *refs):
    pieces, (do_ref, o_ref, k_ref, v_ref, delta_ref, arrived) = refs[: plan.chips], refs[plan.chips :]
    tokens = plan.tokens
    half = tokens // 2
    loads = []
    for n, (source, target) in enumerate(
        ((do_hbm, do_ref), (o_hbm, o_ref), (k_hbm, k_ref), (v_hbm, v_ref))
    ):
        pair = []
        for part in range(2):
            rows = pl.ds(part * half, half)
            copy = pltpu.make_async_copy(source.at[rows], target.at[rows], arrived.at[n, part])
            copy.start()
            pair.append(copy)
        loads.append(pair)

    def wait_for(n):
        for copy in loads[n]:
            copy.wait()

    wait_for(0)
    wait_for(1)
    sums = []
    for head in range(QUERY_HEADS):
        cols = slice(head * HEAD_SIZE, (head + 1) * HEAD_SIZE)
        product = do_ref[:, cols].astype(F32) * o_ref[:, cols].astype(F32)
        sums.append(jnp.sum(product, axis=1, keepdims=True))
    sums.append(jnp.zeros((tokens, LANES - QUERY_HEADS), F32))
    delta_ref[...] = padded_lanes(jnp.concatenate(sums, axis=1).T)
    wait_for(2)
    wait_for(3)
    for mask, out in enumerate(pieces):
        kv_head = plan.first_kv_head(me[0] ^ mask)
        terms = []
        for g in range(plan.q_heads):
            head = kv_head * GROUP + g
            out[g * tokens : (g + 1) * tokens, :] = columns(do_ref, head)[...]
            terms.extend(split3(delta_ref[pl.ds(head, 1), :]))
        for h in range(plan.kv_heads):
            at = plan.q_rows + h * tokens
            out[at : at + tokens, :] = columns(k_ref, kv_head + h)[...]
            at += plan.kv_heads * tokens
            out[at : at + tokens, :] = columns(v_ref, kv_head + h)[...]
        out[plan.q_rows + plan.kv_rows :, :] = padded_rows(terms, plan.aux_sent)


def pack_q_kernel(plan, me, *refs):
    levels, pieces = refs[: -plan.chips], refs[-plan.chips :]
    tokens = plan.tokens
    for mask, out in enumerate(pieces):
        first = plan.first_kv_head(me[0] ^ mask) * GROUP
        for level, ref in enumerate(levels):
            for g in range(plan.q_heads):
                at = level * plan.q_rows + g * tokens
                out[at : at + tokens, :] = columns(ref, first + g)[...]


def stack_kernel(me, *refs):
    pieces, out = refs[:-1], refs[-1]
    rows = pieces[0].shape[0]
    for n, piece in enumerate(pieces):
        out[n * rows : (n + 1) * rows, :] = piece[...]


def assemble_kernel(plan, me, lse_ref, *refs):
    pieces, (do_out, kv_out) = refs[:-2], refs[-2:]
    tokens, split = plan.tokens, plan.q_rows + plan.kv_rows
    for mask, piece in enumerate(pieces):
        chip = me[0] ^ mask
        chunk = (chip % plan.n_x) * CORES + me[1]
        do_out[chip, : plan.q_rows, :] = piece[: plan.q_rows, :]
        kv_out[chip] = piece[plan.q_rows : split, :]
        terms = [piece[split : split + 3 * plan.q_heads, :]]
        for g in range(plan.q_heads):
            if tokens == LANES:
                lanes = pl.ds(pl.multiple_of(chunk * LANES, LANES), LANES)
                row = lse_ref[mask // plan.n_x, pl.ds(g, 1), lanes]
            else:
                row = lse_ref[mask // plan.n_x, chunk, pl.ds(g, 1), :]
            terms.extend(split3(row))
        do_out[chip, plan.q_rows :, :] = padded_rows(terms, plan.aux)


def merge_kernel(groups, me, keep_ref, given_ref, *outs):
    for group, out in zip(groups, outs):
        rows = keep_ref.shape[1]
        for n, mask in enumerate(group):
            chip = me[0] ^ mask
            out[n * rows : (n + 1) * rows, :] = (keep_ref[chip] + given_ref[chip].astype(F32)).astype(BF16)


def lane_row(parts, tokens):
    row = parts[0]
    lane = lax.broadcasted_iota(jnp.int32, row.shape, 1)
    for n, part in enumerate(parts[1:], 1):
        row = jnp.where(lane >= n * tokens, pltpu.roll(part, n * tokens, 1), row)
    return row


def role_kernel(plan, level, has_dq, has_dkv, last, me, code_ref, mine_ref, sib_ref, *refs):
    refs = list(refs)
    q_pieces = [refs.pop(0) for _ in range(plan.chips)]
    do_ref = refs.pop(0)
    dq_in = refs.pop(0) if has_dq else None
    dkv_in = refs.pop(0) if has_dkv else None
    dq_out, dkv_outs, (kv_ref, q_ref, dq_sum, dkv_sum) = refs[0], refs[1:-4], refs[-4:]
    dq_ref = dq_out if dq_out.dtype == F32 else dq_sum
    dkv_ref = dkv_sum if last else dkv_outs[0]
    core = me[1]
    tokens, n_x, fold = plan.tokens, plan.n_x, plan.fold
    q_per = QUERY_TILE // tokens
    k_per = KEY_TILE // tokens
    kv_ref[core] = mine_ref[...]
    kv_ref[1 - core] = sib_ref[...]
    dkv_ref[...] = dkv_in[...] if has_dkv else jnp.zeros_like(dkv_ref)
    dq_ref[...] = dq_in[...] if has_dq else jnp.zeros_like(dq_ref)
    for mask, piece in enumerate(q_pieces):
        q_ref[me[0] ^ mask] = piece[level * plan.q_rows : (level + 1) * plan.q_rows, :]

    def q_start(q_in):
        return (q_in * q_per * CORES + core) * tokens

    def q_end(q_in):
        return ((q_in * q_per + q_per - 1) * CORES + core) * tokens + tokens - 1

    rows_by_rows = (((1,), (1,)), ((), ()))

    def row(query_block, q_in, key_block, k_tiles, code, masked):
        q_chip = query_block * n_x + q_in * q_per
        tile = query_block * plan.q_tiles + q_in

        def q_part(ref, g):
            return [ref[q_chip + n, g * tokens : (g + 1) * tokens, :] for n in range(q_per)]

        def k_place(k_in):
            return [
                (n % CORES, key_block * n_x + k_in * (k_per // CORES) + n // CORES) for n in range(k_per)
            ]

        def k_part(which, h, k_in):
            at = (which * plan.kv_heads + h) * tokens
            return jnp.concatenate([kv_ref[c, chip, at : at + tokens, :] for c, chip in k_place(k_in)], axis=0)

        groups = [do_ref[q_chip + n, plan.q_rows :, :].astype(F32) for n in range(q_per)]

        def aux(which, g):
            at = (which * plan.q_heads + g) * 3
            return lane_row([a[at : at + 1] + a[at + 1 : at + 2] + a[at + 2 : at + 3] for a in groups], tokens)

        queries = []
        for h in range(plan.kv_heads):
            heads = range(h * GROUP, (h + 1) * GROUP)
            q2 = jnp.concatenate([r for g in heads for r in q_part(q_ref, g)], axis=0)
            do2 = jnp.concatenate([r for g in heads for r in q_part(do_ref, g)], axis=0)
            delta = jnp.concatenate([aux(0, g) for g in heads], axis=1)
            lse = jnp.concatenate([aux(1, g) for g in heads], axis=1) * LOG2E
            queries.append((q2, do2, delta, lse))
        units = [(h, k_in) for k_in in k_tiles for h in range(plan.kv_heads)]

        def front(unit):
            h, k_in = unit
            q2, do2, _, _ = queries[h]
            k, v = k_part(0, h, k_in), k_part(1, h, k_in)
            scores = lax.dot_general(k, q2, rows_by_rows, preferred_element_type=F32)
            dprobs = lax.dot_general(v, do2, rows_by_rows, preferred_element_type=F32)
            return k, scores, dprobs

        def back(unit, ready):
            h, k_in = unit
            q2, do2, delta, lse = queries[h]
            k, scores, dprobs = ready
            probs = jnp.exp2(scores * (SCALE * LOG2E) - lse)
            if masked:
                key_at = lax.broadcasted_iota(jnp.int32, probs.shape, 0) + k_in * KEY_TILE
                lane = lax.broadcasted_iota(jnp.int32, probs.shape, 1) % QUERY_TILE
                query_at = q_start(q_in) + lane % tokens + (lane // tokens) * (CORES * tokens)
                ahead = key_at - query_at
                allowed = jnp.where(code == 2, ahead, 1 - ahead) <= 0
                probs = jnp.where(allowed, probs, 0.0)
            dscores = (probs * (dprobs - delta) * SCALE).astype(BF16)
            dv = jnp.dot(probs.astype(BF16), do2, preferred_element_type=F32)
            dk = jnp.dot(dscores, q2, preferred_element_type=F32)
            for n, (c, chip) in enumerate(k_place(k_in)):
                rows = slice(n * tokens, (n + 1) * tokens)
                at = h * tokens
                dkv_ref[c, chip, at : at + tokens, :] += dk[rows]
                at += plan.kv_heads * tokens
                dkv_ref[c, chip, at : at + tokens, :] += dv[rows]
            return jnp.dot(k.T, dscores, preferred_element_type=F32)

        ready = front(units[0])
        for n, unit in enumerate(units):
            following = front(units[n + 1]) if n + 1 < len(units) else None
            dq_ref[tile, unit[0]] += back(unit, ready)
            ready = following

    def step(index, carry):
        q_in = index % plan.q_tiles
        rest = index // plan.q_tiles
        key_block = rest % fold
        query_block = rest // fold
        code = code_ref[query_block, key_block]
        q_first, q_last = q_start(q_in), q_end(q_in)
        every = tuple(range(plan.k_tiles))
        below = (q_last < (plan.k_tiles - 1) * KEY_TILE) & (code == 2)
        above = (q_first >= KEY_TILE - 1) & (code == 3)

        @pl.when(code == 1)
        def _():
            row(query_block, q_in, key_block, every, code, False)

        @pl.when(below | above)
        def _():
            row(query_block, q_in, key_block, (jnp.where(below, 0, plan.k_tiles - 1),), code, True)

        @pl.when((code >= 2) & jnp.logical_not(below | above))
        def _():
            row(query_block, q_in, key_block, every, code, True)

        return carry

    lax.fori_loop(0, fold * fold * plan.q_tiles, step, 0)
    if dq_out.dtype != F32:
        dq_out[...] = dq_ref[...].astype(dq_out.dtype)
    if last:
        keep, give = dkv_outs
        keep[...] = dkv_ref[core]
        give[...] = dkv_ref[1 - core].astype(BF16)


def finish_kernel(plan, has_far, me, dq_ref, *refs):
    refs = list(refs)
    far_ref = refs.pop(0) if has_far else None
    pieces, rows_ref = refs[:-1], refs[-1]
    tokens = plan.tokens
    q_per = QUERY_TILE // tokens
    for tile in range(dq_ref.shape[0]):
        for h in range(plan.kv_heads):
            total = dq_ref[tile, h]
            if has_far:
                total = total + far_ref[tile, h].astype(F32)
            turned = total.T.astype(BF16)
            for g in range(GROUP):
                for n in range(q_per):
                    at = (h * GROUP + g) * tokens
                    source = g * QUERY_TILE + n * tokens
                    rows_ref[tile * q_per + n, at : at + tokens, :] = turned[source : source + tokens]
    for mask, out in enumerate(pieces):
        out[...] = rows_ref[me[0] ^ mask]


def unpack_kernel(plan, levels, me, *refs):
    refs = list(refs)
    direct, by_way = routes(plan.chips)
    dq_pieces = [refs.pop(0) for _ in range(plan.chips)]
    near = [refs.pop(0) for _ in range(plan.chips)]
    far = {mask: [] for mask in range(plan.chips)}
    for _ in range(levels - 1):
        for mask in direct:
            far[mask].append((refs.pop(0), 0))
        both = refs.pop(0)
        for n, mask in enumerate(by_way):
            far[mask].append((both, n * plan.kv_rows))
    dq_ref, dk_ref, dv_ref = refs
    tokens = plan.tokens
    for mask in range(plan.chips):
        kv_head = plan.first_kv_head(me[0] ^ mask)
        for g in range(plan.q_heads):
            columns(dq_ref, kv_head * GROUP + g)[...] = dq_pieces[mask][g * tokens : (g + 1) * tokens, :]
        total = near[mask][...]
        if far[mask]:
            total = total.astype(F32)
            for ref, at in far[mask]:
                total = total + ref[at : at + plan.kv_rows, :].astype(F32)
            total = total.astype(BF16)
        for h in range(plan.kv_heads):
            columns(dk_ref, kv_head + h)[...] = total[h * tokens : (h + 1) * tokens]
            at = (plan.kv_heads + h) * tokens
            columns(dv_ref, kv_head + h)[...] = total[at : at + tokens]


def routes(chips):
    by_way = [mask for mask in range(chips) if mask.bit_count() == 1]
    return [mask for mask in range(chips) if mask not in by_way], by_way


def send_in_plane(piece, mask, chips):
    if mask == 0:
        return piece
    return lax.ppermute(piece, CROSS, [(i, i ^ mask) for i in range(chips)])


def exchange(pieces):
    return [send_in_plane(piece, mask, len(pieces)) for mask, piece in enumerate(pieces)]


def swap(value):
    return lax.ppermute(value, "core", [(0, 1), (1, 0)])


def along(value, planes, steps):
    pairs = [(i, i + steps) for i in range(planes) if 0 <= i + steps < planes]
    return lax.ppermute(value, "z", pairs)


def query_levels(level, reach):
    return [d - level for d in (2 * level, 2 * level - 1) if 0 <= d <= reach]


def plane_logsum(logsum, plan, y, core):
    blocks = [logsum]
    for mask in range(1, plan.fold):
        blocks.append(lax.ppermute(logsum, "y", [(i, i ^ mask) for i in range(plan.fold)]))
    mine = jnp.stack(blocks)
    other = swap(mine)
    both = jnp.where(core == 0, jnp.concatenate([mine, other], axis=1), jnp.concatenate([other, mine], axis=1))
    lse = lax.dynamic_slice_in_dim(both, y * plan.q_heads, plan.q_heads, axis=1)
    if plan.tokens == LANES:
        return lse
    lse = lse.reshape(plan.fold, plan.q_heads, plan.n_x * CORES, plan.tokens).transpose(0, 2, 1, 3)
    return jnp.pad(lse, ((0, 0), (0, 0), (0, 0), (0, LANES - plan.tokens)))


def body(queries, output_gradient, outputs, key_vectors, values, logsum, pair_list):
    planes, fold, n_x = (lax.axis_size(a) for a in ("z", "y", "x"))
    plan = Plan(fold, n_x, queries.shape[0])
    chips = plan.chips
    reach = -(-(WIN - 1) // fold)
    z, y, core = (lax.axis_index(a) for a in ("z", "y", "core"))

    def like(rows):
        return jax.ShapeDtypeStruct((rows, LANES), BF16)

    def stacked(rows, dtype=BF16):
        return jax.ShapeDtypeStruct((chips, rows, LANES), dtype)

    raw = [queries]
    for _ in range(1, reach // 2 + 1):
        raw.append(along(raw[-1], planes, -1))

    lse = plane_logsum(logsum, plan, y, core)
    arrays = (output_gradient, outputs, key_vectors, values)
    pieces = call(
        functools.partial(pack_kernel, plan),
        [like(plan.q_rows + plan.kv_rows + plan.aux_sent)] * chips,
        [pl.BlockSpec(memory_space=pltpu.HBM)] * len(arrays),
        scratch=[pltpu.VMEM(a.shape, a.dtype) for a in arrays]
        + [pltpu.VMEM((LANES, LANES), F32), pltpu.SemaphoreType.DMA((len(arrays), 2))],
        vmem=60 * 1024 * 1024,
    )(*arrays)
    do_own, kv_own = call(
        functools.partial(assemble_kernel, plan),
        [stacked(plan.q_rows + plan.aux), stacked(plan.kv_rows)],
        [WHOLE] * (chips + 1),
    )(lse, *exchange(pieces))

    up = [kv_own]
    for _ in range(1, (reach + 1) // 2 + 1):
        up.append(along(up[-1], planes, 1))
    far_do = [do_own]
    for _ in range(1, reach // 2 + 1):
        far_do.append(along(far_do[-1], planes, -1))
    q_pieces = exchange(
        call(functools.partial(pack_q_kernel, plan), [like(len(raw) * plan.q_rows)] * chips, [WHOLE] * len(raw))(*raw),
    )
    up = [(kv, swap(kv)) for kv in up]

    grad_q = [None] * len(raw)
    near_kv, far_kv = None, []
    dq_shape = (fold * plan.q_tiles, plan.kv_heads, HEAD_SIZE, GROUP * QUERY_TILE)
    dkv_shape = (CORES, chips, plan.kv_rows, LANES)
    inside = jnp.arange(fold, dtype=jnp.int32)
    cases = [(i, j) for i in range(len(up)) for j in query_levels(i, reach)]
    query_blocks = (z + jnp.array([j for _, j in cases], jnp.int32)[:, None]) * fold + inside
    key_blocks = (z - jnp.array([i for i, _ in cases], jnp.int32)[:, None]) * fold + inside
    listed = pair_list[:, :, None, None, None]
    hit = (listed[:, 0] == query_blocks[:, :, None]) & (listed[:, 1] == key_blocks[:, None, :])
    codes = jnp.sum(jnp.where(hit, listed[:, 2] + 1, 0), axis=0).astype(jnp.int32)
    direct, by_way = routes(chips)
    for i, (mine, sibling) in enumerate(up):
        levels = query_levels(i, reach)
        carried = None
        for j in levels:
            has_dq, last = grad_q[j] is not None, j == levels[-1]
            done = j and j not in query_levels(i + 1, reach)
            dkv_outs = (
                [stacked(plan.kv_rows, F32), stacked(plan.kv_rows)]
                if last
                else [jax.ShapeDtypeStruct(dkv_shape, F32)]
            )
            given = [g for g in (grad_q[j], carried) if g is not None]
            grad_q[j], *dkv = call(
                functools.partial(role_kernel, plan, j, has_dq, carried is not None, last),
                [jax.ShapeDtypeStruct(dq_shape, BF16 if done else F32)] + dkv_outs,
                [SCALARS] + [WHOLE] * (3 + chips + len(given)),
                flops=10 * fold * fold * plan.q_heads * plan.block * plan.block * HEAD_SIZE // CORES,
                scratch=[
                    pltpu.VMEM(dkv_shape, BF16),
                    pltpu.VMEM((chips, plan.q_rows, LANES), BF16),
                    pltpu.VMEM(dq_shape, F32),
                    pltpu.VMEM(dkv_shape, F32),
                ],
            )(codes[cases.index((i, j))], mine, sibling, *q_pieces, far_do[j], *given)
            carried = dkv[0]
        keep, give = dkv
        groups = [direct] + [[m] for m in by_way] if i else [[m] for m in range(chips)]
        merged = call(
            functools.partial(merge_kernel, groups), [like(len(group) * plan.kv_rows) for group in groups], [WHOLE] * 2
        )(keep, swap(give))
        if i == 0:
            near_kv = exchange(merged)
            continue
        first = along(merged[0], planes, -i)
        for n, mask in enumerate(direct):
            piece = first[n * plan.kv_rows : (n + 1) * plan.kv_rows]
            far_kv.append(send_in_plane(piece, mask, chips))
        pair = [send_in_plane(p, m, chips) for p, m in zip(merged[1:], by_way)]
        both = call(stack_kernel, like(len(by_way) * plan.kv_rows), [WHOLE] * len(by_way))(*pair)
        far_kv.append(along(both, planes, -i))

    def plus(part, far):
        return part if far is None else (part.astype(F32) + far.astype(F32)).astype(BF16)

    far_q = None
    for level in range(len(grad_q) - 1, 0, -1):
        far_q = along(plus(grad_q[level], far_q), planes, 1)
    dq_pieces = call(
        functools.partial(finish_kernel, plan, far_q is not None),
        [like(plan.q_rows)] * chips,
        [WHOLE] + [WHOLE] * (far_q is not None),
        scratch=[pltpu.VMEM((chips, plan.q_rows, LANES), BF16)],
    )(grad_q[0], *([] if far_q is None else [far_q]))
    return tuple(
        call(
            functools.partial(unpack_kernel, plan, len(up)),
            [
                jax.ShapeDtypeStruct((plan.tokens, QUERY_HEADS * HEAD_SIZE), BF16),
                jax.ShapeDtypeStruct((plan.tokens, KEY_VALUE_HEADS * HEAD_SIZE), BF16),
                jax.ShapeDtypeStruct((plan.tokens, KEY_VALUE_HEADS * HEAD_SIZE), BF16),
            ],
            [WHOLE] * (2 * chips + len(far_kv)),
        )(*exchange(dq_pieces), *near_kv, *far_kv)
    )


def solution(mesh):
    n_seq, n_head = mesh.shape["seq"], mesh.shape["head"]
    fold = KEY_VALUE_HEADS // n_head
    assert n_head * fold == KEY_VALUE_HEADS and n_seq % fold == 0 and n_head % CORES == 0
    names = ("z", "y", "x", "core")
    planes = Mesh(mesh.devices.reshape(n_seq // fold, fold, n_head // CORES, CORES), names)
    rows = P(names, None)
    return jax.shard_map(
        body,
        mesh=planes,
        in_specs=(rows,) * 5 + (P(("x", "core"), ("z", "y")), P()),
        out_specs=(rows,) * 3,
        check_vma=False,
    )
```

```python
import functools
import math

import jax
import jax.numpy as jnp
from jax import lax
from jax.experimental import pallas as pl
from jax.experimental.pallas import tpu as pltpu
from jax.sharding import Mesh, PartitionSpec as P


HEAD_SIZE = 128
KEY_VALUE_HEADS = 8
QUERY_HEADS = 16
WIN = 5
GROUP = QUERY_HEADS // KEY_VALUE_HEADS
CORES = 2
KEY_TILE = 256
QUERY_TILE = 128
LANES = 128
PACK = 16
LOG2E = math.log2(math.e)
SCALE = 1.0 / math.sqrt(HEAD_SIZE)
BF16 = jnp.bfloat16
F32 = jnp.float32
CROSS = ("y", "x")
WHOLE = pl.BlockSpec(memory_space=pltpu.VMEM)
IN_HBM = pl.BlockSpec(memory_space=pltpu.HBM)
SCALARS = pl.BlockSpec(memory_space=pltpu.SMEM)
VMEM_BYTES = 16 * 1024 * 1024


def call(kernel, out_shape, in_specs, flops=0, moved=4 << 20, scratch=()):
    def placed(*refs):
        n_x = lax.axis_size("x")
        return kernel((lax.axis_index("y") * n_x + lax.axis_index("x"), lax.axis_index("core")), *refs)

    return pl.pallas_call(
        placed,
        out_shape=out_shape,
        in_specs=in_specs,
        out_specs=jax.tree.map(lambda _: WHOLE, out_shape),
        scratch_shapes=scratch,
        cost_estimate=pl.CostEstimate(flops=flops, bytes_accessed=moved, transcendentals=0),
        compiler_params=pltpu.CompilerParams(vmem_limit_bytes=VMEM_BYTES),
    )


def split3(x):
    hi = x.astype(BF16)
    rest = x - hi.astype(F32)
    mid = rest.astype(BF16)
    low = (rest - mid.astype(F32)).astype(BF16)
    return hi, mid, low


def round_up(n, to):
    return -(-n // to) * to


class Plan:
    def __init__(self, fold, n_x, tokens):
        self.fold, self.n_x, self.tokens = fold, n_x, tokens
        self.chips = fold * n_x
        self.kv_heads = KEY_VALUE_HEADS // self.chips
        self.q_heads = self.kv_heads * GROUP
        self.block = n_x * CORES * tokens
        self.q_rows = self.q_heads * tokens
        self.kv_rows = 2 * self.kv_heads * tokens
        self.aux_sent = round_up(3 * self.q_heads, PACK)
        self.aux = round_up(6 * self.q_heads, PACK)
        self.q_tiles = n_x * tokens // QUERY_TILE
        self.k_tiles = self.block // KEY_TILE
        assert self.k_tiles == 2

    def first_kv_head(self, chip):
        return ((chip % self.n_x) * self.fold + chip // self.n_x) * self.kv_heads


def columns(ref, head):
    return ref.at[:, pl.ds(pl.multiple_of(head * HEAD_SIZE, LANES), HEAD_SIZE)]


def padded_lanes(x):
    rows, width = x.shape
    if width == LANES:
        return x
    return jnp.concatenate([x, jnp.zeros((rows, LANES - width), x.dtype)], axis=1)


def padded_rows(terms, rows):
    have = sum(t.shape[0] for t in terms)
    if have < rows:
        terms = terms + [jnp.zeros((rows - have, LANES), BF16)]
    return jnp.concatenate(terms, axis=0)


def load(arrived, pairs):
    started = []
    for n, (source, target) in enumerate(pairs):
        half = target.shape[0] // 2
        halves = []
        for part in range(2):
            rows = pl.ds(part * half, half)
            copy = pltpu.make_async_copy(source.at[rows], target.at[rows], arrived.at[n, part])
            copy.start()
            halves.append(copy)
        started.append(halves)

    def wait_for(n):
        for copy in started[n]:
            copy.wait()

    return wait_for


def pack_kernel(plan, me, do_hbm, o_hbm, k_hbm, v_hbm, *refs):
    pieces, (do_ref, o_ref, k_ref, v_ref, delta_ref, arrived) = refs[: plan.chips], refs[plan.chips :]
    tokens = plan.tokens
    wait_for = load(arrived, ((do_hbm, do_ref), (o_hbm, o_ref), (k_hbm, k_ref), (v_hbm, v_ref)))
    wait_for(0)
    wait_for(1)
    sums = []
    for head in range(QUERY_HEADS):
        cols = slice(head * HEAD_SIZE, (head + 1) * HEAD_SIZE)
        product = do_ref[:, cols].astype(F32) * o_ref[:, cols].astype(F32)
        sums.append(jnp.sum(product, axis=1, keepdims=True))
    sums.append(jnp.zeros((tokens, LANES - QUERY_HEADS), F32))
    delta_ref[...] = padded_lanes(jnp.concatenate(sums, axis=1).T)
    wait_for(2)
    wait_for(3)
    for mask, out in enumerate(pieces):
        kv_head = plan.first_kv_head(me[0] ^ mask)
        terms = []
        for g in range(plan.q_heads):
            head = kv_head * GROUP + g
            out[g * tokens : (g + 1) * tokens, :] = columns(do_ref, head)[...]
            terms.extend(split3(delta_ref[pl.ds(head, 1), :]))
        for h in range(plan.kv_heads):
            at = plan.q_rows + h * tokens
            out[at : at + tokens, :] = columns(k_ref, kv_head + h)[...]
            at += plan.kv_heads * tokens
            out[at : at + tokens, :] = columns(v_ref, kv_head + h)[...]
        out[plan.q_rows + plan.kv_rows :, :] = padded_rows(terms, plan.aux_sent)


def pack_q_kernel(plan, me, own_hbm, *refs):
    own_ref, arrived = refs[-2:]
    above, pieces = refs[: -plan.chips - 2], refs[-plan.chips - 2 : -2]
    tokens = plan.tokens
    wait_for = load(arrived, ((own_hbm, own_ref),))
    for level, ref in reversed(list(enumerate((own_ref,) + above))):
        if level == 0:
            wait_for(0)
        for mask, out in enumerate(pieces):
            first = plan.first_kv_head(me[0] ^ mask) * GROUP
            for g in range(plan.q_heads):
                at = level * plan.q_rows + g * tokens
                out[at : at + tokens, :] = columns(ref, first + g)[...]


def stack_kernel(me, *refs):
    pieces, out = refs[:-1], refs[-1]
    rows = pieces[0].shape[0]
    for n, piece in enumerate(pieces):
        out[n * rows : (n + 1) * rows, :] = piece[...]


def assemble_kernel(plan, me, lse_ref, *refs):
    pieces, (do_out, kv_out) = refs[:-2], refs[-2:]
    tokens, split = plan.tokens, plan.q_rows + plan.kv_rows
    for mask, piece in enumerate(pieces):
        chip = me[0] ^ mask
        chunk = (chip % plan.n_x) * CORES + me[1]
        do_out[chip, : plan.q_rows, :] = piece[: plan.q_rows, :]
        kv_out[chip] = piece[plan.q_rows : split, :]
        terms = [piece[split : split + 3 * plan.q_heads, :]]
        for g in range(plan.q_heads):
            if tokens == LANES:
                lanes = pl.ds(pl.multiple_of(chunk * LANES, LANES), LANES)
                row = lse_ref[mask // plan.n_x, pl.ds(g, 1), lanes]
            else:
                row = lse_ref[mask // plan.n_x, chunk, pl.ds(g, 1), :]
            terms.extend(split3(row))
        do_out[chip, plan.q_rows :, :] = padded_rows(terms, plan.aux)


def merge_kernel(groups, me, keep_ref, given_ref, *outs):
    for group, out in zip(groups, outs):
        rows = keep_ref.shape[1]
        for n, mask in enumerate(group):
            chip = me[0] ^ mask
            out[n * rows : (n + 1) * rows, :] = (keep_ref[chip] + given_ref[chip].astype(F32)).astype(BF16)


def lane_row(parts, tokens):
    row = parts[0]
    lane = lax.broadcasted_iota(jnp.int32, row.shape, 1)
    for n, part in enumerate(parts[1:], 1):
        row = jnp.where(lane >= n * tokens, pltpu.roll(part, n * tokens, 1), row)
    return row


def role_kernel(plan, level, has_dq, has_dkv, last, me, code_ref, mine_ref, sib_ref, *refs):
    refs = list(refs)
    q_pieces = [refs.pop(0) for _ in range(plan.chips)]
    do_ref = refs.pop(0)
    dq_in = refs.pop(0) if has_dq else None
    dkv_in = refs.pop(0) if has_dkv else None
    dq_out, dkv_outs, (kv_ref, q_ref, dq_sum, dkv_sum) = refs[0], refs[1:-4], refs[-4:]
    dq_ref = dq_out if dq_out.dtype == F32 else dq_sum
    dkv_ref = dkv_sum if last else dkv_outs[0]
    core = me[1]
    tokens, n_x, fold = plan.tokens, plan.n_x, plan.fold
    q_per = QUERY_TILE // tokens
    k_per = KEY_TILE // tokens
    kv_ref[core] = mine_ref[...]
    kv_ref[1 - core] = sib_ref[...]
    dkv_ref[...] = dkv_in[...] if has_dkv else jnp.zeros_like(dkv_ref)
    dq_ref[...] = dq_in[...] if has_dq else jnp.zeros_like(dq_ref)
    for mask, piece in enumerate(q_pieces):
        q_ref[me[0] ^ mask] = piece[level * plan.q_rows : (level + 1) * plan.q_rows, :]

    def q_start(q_in):
        return (q_in * q_per * CORES + core) * tokens

    def q_end(q_in):
        return ((q_in * q_per + q_per - 1) * CORES + core) * tokens + tokens - 1

    rows_by_rows = (((1,), (1,)), ((), ()))

    def row(query_block, q_in, key_block, k_tiles, code, masked):
        q_chip = query_block * n_x + q_in * q_per
        tile = query_block * plan.q_tiles + q_in

        def q_part(ref, g):
            return [ref[q_chip + n, g * tokens : (g + 1) * tokens, :] for n in range(q_per)]

        def k_place(k_in):
            return [
                (n % CORES, key_block * n_x + k_in * (k_per // CORES) + n // CORES) for n in range(k_per)
            ]

        def k_part(which, h, k_in):
            at = (which * plan.kv_heads + h) * tokens
            return jnp.concatenate([kv_ref[c, chip, at : at + tokens, :] for c, chip in k_place(k_in)], axis=0)

        groups = [do_ref[q_chip + n, plan.q_rows :, :].astype(F32) for n in range(q_per)]

        def aux(which, g):
            at = (which * plan.q_heads + g) * 3
            return lane_row([a[at : at + 1] + a[at + 1 : at + 2] + a[at + 2 : at + 3] for a in groups], tokens)

        queries = []
        for h in range(plan.kv_heads):
            heads = range(h * GROUP, (h + 1) * GROUP)
            q2 = jnp.concatenate([r for g in heads for r in q_part(q_ref, g)], axis=0)
            do2 = jnp.concatenate([r for g in heads for r in q_part(do_ref, g)], axis=0)
            delta = jnp.concatenate([aux(0, g) for g in heads], axis=1)
            lse = jnp.concatenate([aux(1, g) for g in heads], axis=1) * LOG2E
            queries.append((q2, do2, delta, lse))
        units = [(h, k_in) for k_in in k_tiles for h in range(plan.kv_heads)]

        def front(unit):
            h, k_in = unit
            q2, do2, _, _ = queries[h]
            k, v = k_part(0, h, k_in), k_part(1, h, k_in)
            scores = lax.dot_general(k, q2, rows_by_rows, preferred_element_type=F32)
            dprobs = lax.dot_general(v, do2, rows_by_rows, preferred_element_type=F32)
            return k, scores, dprobs

        def back(unit, ready):
            h, k_in = unit
            q2, do2, delta, lse = queries[h]
            k, scores, dprobs = ready
            probs = jnp.exp2(scores * (SCALE * LOG2E) - lse)
            if masked:
                key_at = lax.broadcasted_iota(jnp.int32, probs.shape, 0) + k_in * KEY_TILE
                lane = lax.broadcasted_iota(jnp.int32, probs.shape, 1) % QUERY_TILE
                query_at = q_start(q_in) + lane % tokens + (lane // tokens) * (CORES * tokens)
                ahead = key_at - query_at
                allowed = jnp.where(code == 2, ahead, 1 - ahead) <= 0
                probs = jnp.where(allowed, probs, 0.0)
            dscores = (probs * (dprobs - delta) * SCALE).astype(BF16)
            dv = jnp.dot(probs.astype(BF16), do2, preferred_element_type=F32)
            dk = jnp.dot(dscores, q2, preferred_element_type=F32)
            for n, (c, chip) in enumerate(k_place(k_in)):
                rows = slice(n * tokens, (n + 1) * tokens)
                at = h * tokens
                dkv_ref[c, chip, at : at + tokens, :] += dk[rows]
                at += plan.kv_heads * tokens
                dkv_ref[c, chip, at : at + tokens, :] += dv[rows]
            return jnp.dot(k.T, dscores, preferred_element_type=F32)

        ready = front(units[0])
        for n, unit in enumerate(units):
            following = front(units[n + 1]) if n + 1 < len(units) else None
            dq_ref[tile, unit[0]] += back(unit, ready)
            ready = following

    def step(index, carry):
        q_in = index % plan.q_tiles
        rest = index // plan.q_tiles
        key_block = rest % fold
        query_block = rest // fold
        code = code_ref[query_block, key_block]
        q_first, q_last = q_start(q_in), q_end(q_in)
        every = tuple(range(plan.k_tiles))
        below = (q_last < (plan.k_tiles - 1) * KEY_TILE) & (code == 2)
        above = (q_first >= KEY_TILE - 1) & (code == 3)

        @pl.when(code == 1)
        def _():
            row(query_block, q_in, key_block, every, code, False)

        @pl.when(below | above)
        def _():
            row(query_block, q_in, key_block, (jnp.where(below, 0, plan.k_tiles - 1),), code, True)

        @pl.when((code >= 2) & jnp.logical_not(below | above))
        def _():
            row(query_block, q_in, key_block, every, code, True)

        return carry

    lax.fori_loop(0, fold * fold * plan.q_tiles, step, 0)
    if dq_out.dtype != F32:
        dq_out[...] = dq_ref[...].astype(dq_out.dtype)
    if last:
        keep, give = dkv_outs
        keep[...] = dkv_ref[core]
        give[...] = dkv_ref[1 - core].astype(BF16)


def finish_kernel(plan, has_far, me, dq_ref, *refs):
    refs = list(refs)
    far_ref = refs.pop(0) if has_far else None
    pieces, rows_ref = refs[:-1], refs[-1]
    tokens = plan.tokens
    q_per = QUERY_TILE // tokens
    for tile in range(dq_ref.shape[0]):
        for h in range(plan.kv_heads):
            total = dq_ref[tile, h]
            if has_far:
                total = total + far_ref[tile, h].astype(F32)
            turned = total.T.astype(BF16)
            for g in range(GROUP):
                for n in range(q_per):
                    at = (h * GROUP + g) * tokens
                    source = g * QUERY_TILE + n * tokens
                    rows_ref[tile * q_per + n, at : at + tokens, :] = turned[source : source + tokens]
    for mask, out in enumerate(pieces):
        out[...] = rows_ref[me[0] ^ mask]


def unpack_kernel(plan, levels, me, *refs):
    refs = list(refs)
    direct, by_way = routes(plan.chips)
    dq_pieces = [refs.pop(0) for _ in range(plan.chips)]
    near = [refs.pop(0) for _ in range(plan.chips)]
    far = {mask: [] for mask in range(plan.chips)}
    for _ in range(levels - 1):
        for mask in direct:
            far[mask].append((refs.pop(0), 0))
        both = refs.pop(0)
        for n, mask in enumerate(by_way):
            far[mask].append((both, n * plan.kv_rows))
    dq_ref, dk_ref, dv_ref = refs
    tokens = plan.tokens
    for mask in range(plan.chips):
        kv_head = plan.first_kv_head(me[0] ^ mask)
        for g in range(plan.q_heads):
            columns(dq_ref, kv_head * GROUP + g)[...] = dq_pieces[mask][g * tokens : (g + 1) * tokens, :]
        total = near[mask][...]
        if far[mask]:
            total = total.astype(F32)
            for ref, at in far[mask]:
                total = total + ref[at : at + plan.kv_rows, :].astype(F32)
            total = total.astype(BF16)
        for h in range(plan.kv_heads):
            columns(dk_ref, kv_head + h)[...] = total[h * tokens : (h + 1) * tokens]
            at = (plan.kv_heads + h) * tokens
            columns(dv_ref, kv_head + h)[...] = total[at : at + tokens]


def routes(chips):
    by_way = [mask for mask in range(chips) if mask.bit_count() == 1]
    return [mask for mask in range(chips) if mask not in by_way], by_way


def send_in_plane(piece, mask, chips):
    if mask == 0:
        return piece
    return lax.ppermute(piece, CROSS, [(i, i ^ mask) for i in range(chips)])


def exchange(pieces):
    return [send_in_plane(piece, mask, len(pieces)) for mask, piece in enumerate(pieces)]


def swap(value):
    return lax.ppermute(value, "core", [(0, 1), (1, 0)])


def along(value, planes, steps):
    pairs = [(i, i + steps) for i in range(planes) if 0 <= i + steps < planes]
    return lax.ppermute(value, "z", pairs)


def query_levels(level, reach):
    return [d - level for d in (2 * level, 2 * level - 1) if 0 <= d <= reach]


def plane_logsum(logsum, plan, y, core):
    blocks = [logsum]
    for mask in range(1, plan.fold):
        blocks.append(lax.ppermute(logsum, "y", [(i, i ^ mask) for i in range(plan.fold)]))
    mine = jnp.stack(blocks)
    other = swap(mine)
    both = jnp.where(core == 0, jnp.concatenate([mine, other], axis=1), jnp.concatenate([other, mine], axis=1))
    lse = lax.dynamic_slice_in_dim(both, y * plan.q_heads, plan.q_heads, axis=1)
    if plan.tokens == LANES:
        return lse
    lse = lse.reshape(plan.fold, plan.q_heads, plan.n_x * CORES, plan.tokens).transpose(0, 2, 1, 3)
    return jnp.pad(lse, ((0, 0), (0, 0), (0, 0), (0, LANES - plan.tokens)))


def body(queries, output_gradient, outputs, key_vectors, values, logsum, pair_list):
    planes, fold, n_x = (lax.axis_size(a) for a in ("z", "y", "x"))
    plan = Plan(fold, n_x, queries.shape[0])
    chips = plan.chips
    reach = -(-(WIN - 1) // fold)
    z, y, core = (lax.axis_index(a) for a in ("z", "y", "core"))

    def like(rows):
        return jax.ShapeDtypeStruct((rows, LANES), BF16)

    def stacked(rows, dtype=BF16):
        return jax.ShapeDtypeStruct((chips, rows, LANES), dtype)

    kept = functools.partial(pltpu.with_memory_space_constraint, memory_space=pltpu.HBM)
    raw = [queries]
    for _ in range(1, reach // 2 + 1):
        raw.append(along(raw[-1], planes, -1))

    lse = plane_logsum(logsum, plan, y, core)
    arrays = (output_gradient, outputs, key_vectors, values)
    pieces = call(
        functools.partial(pack_kernel, plan),
        [like(plan.q_rows + plan.kv_rows + plan.aux_sent)] * chips,
        [IN_HBM] * len(arrays),
        scratch=[pltpu.VMEM(a.shape, a.dtype) for a in arrays]
        + [pltpu.VMEM((LANES, LANES), F32), pltpu.SemaphoreType.DMA((len(arrays), 2))],
    )(*map(kept, arrays))
    do_own, kv_own = call(
        functools.partial(assemble_kernel, plan),
        [stacked(plan.q_rows + plan.aux), stacked(plan.kv_rows)],
        [WHOLE] * (chips + 1),
    )(lse, *exchange(pieces))

    up = [kv_own]
    for _ in range(1, (reach + 1) // 2 + 1):
        up.append(along(up[-1], planes, 1))
    far_do = [do_own]
    for _ in range(1, reach // 2 + 1):
        far_do.append(along(far_do[-1], planes, -1))
    q_pieces = exchange(
        call(
            functools.partial(pack_q_kernel, plan),
            [like(len(raw) * plan.q_rows)] * chips,
            [IN_HBM] + [WHOLE] * (len(raw) - 1),
            scratch=[pltpu.VMEM(queries.shape, BF16), pltpu.SemaphoreType.DMA((1, 2))],
        )(kept(queries), *raw[1:]),
    )
    up = [(kv, swap(kv)) for kv in up]

    grad_q = [None] * len(raw)
    near_kv, far_kv = None, []
    dq_shape = (fold * plan.q_tiles, plan.kv_heads, HEAD_SIZE, GROUP * QUERY_TILE)
    dkv_shape = (CORES, chips, plan.kv_rows, LANES)
    inside = jnp.arange(fold, dtype=jnp.int32)
    cases = [(i, j) for i in range(len(up)) for j in query_levels(i, reach)]
    query_blocks = (z + jnp.array([j for _, j in cases], jnp.int32)[:, None]) * fold + inside
    key_blocks = (z - jnp.array([i for i, _ in cases], jnp.int32)[:, None]) * fold + inside
    listed = pair_list[:, :, None, None, None]
    hit = (listed[:, 0] == query_blocks[:, :, None]) & (listed[:, 1] == key_blocks[:, None, :])
    codes = jnp.sum(jnp.where(hit, listed[:, 2] + 1, 0), axis=0).astype(jnp.int32)
    direct, by_way = routes(chips)
    for i, (mine, sibling) in enumerate(up):
        levels = query_levels(i, reach)
        carried = None
        for j in levels:
            has_dq, last = grad_q[j] is not None, j == levels[-1]
            done = j and j not in query_levels(i + 1, reach)
            dkv_outs = (
                [stacked(plan.kv_rows, F32), stacked(plan.kv_rows)]
                if last
                else [jax.ShapeDtypeStruct(dkv_shape, F32)]
            )
            given = [g for g in (grad_q[j], carried) if g is not None]
            grad_q[j], *dkv = call(
                functools.partial(role_kernel, plan, j, has_dq, carried is not None, last),
                [jax.ShapeDtypeStruct(dq_shape, BF16 if done else F32)] + dkv_outs,
                [SCALARS] + [WHOLE] * (3 + chips + len(given)),
                flops=10 * fold * fold * plan.q_heads * plan.block * plan.block * HEAD_SIZE // CORES,
                scratch=[
                    pltpu.VMEM(dkv_shape, BF16),
                    pltpu.VMEM((chips, plan.q_rows, LANES), BF16),
                    pltpu.VMEM(dq_shape, F32),
                    pltpu.VMEM(dkv_shape, F32),
                ],
            )(codes[cases.index((i, j))], mine, sibling, *q_pieces, far_do[j], *given)
            carried = dkv[0]
        keep, give = dkv
        groups = [direct] + [[m] for m in by_way] if i else [[m] for m in range(chips)]
        merged = call(
            functools.partial(merge_kernel, groups), [like(len(group) * plan.kv_rows) for group in groups], [WHOLE] * 2
        )(keep, swap(give))
        if i == 0:
            near_kv = exchange(merged)
            continue
        first = along(merged[0], planes, -i)
        for n, mask in enumerate(direct):
            piece = first[n * plan.kv_rows : (n + 1) * plan.kv_rows]
            far_kv.append(send_in_plane(piece, mask, chips))
        pair = [send_in_plane(p, m, chips) for p, m in zip(merged[1:], by_way)]
        both = call(stack_kernel, like(len(by_way) * plan.kv_rows), [WHOLE] * len(by_way))(*pair)
        far_kv.append(along(both, planes, -i))

    def plus(part, far):
        return part if far is None else (part.astype(F32) + far.astype(F32)).astype(BF16)

    far_q = None
    for level in range(len(grad_q) - 1, 0, -1):
        far_q = along(plus(grad_q[level], far_q), planes, 1)
    dq_pieces = call(
        functools.partial(finish_kernel, plan, far_q is not None),
        [like(plan.q_rows)] * chips,
        [WHOLE] + [WHOLE] * (far_q is not None),
        scratch=[pltpu.VMEM((chips, plan.q_rows, LANES), BF16)],
    )(grad_q[0], *([] if far_q is None else [far_q]))
    return tuple(
        call(
            functools.partial(unpack_kernel, plan, len(up)),
            [
                jax.ShapeDtypeStruct((plan.tokens, QUERY_HEADS * HEAD_SIZE), BF16),
                jax.ShapeDtypeStruct((plan.tokens, KEY_VALUE_HEADS * HEAD_SIZE), BF16),
                jax.ShapeDtypeStruct((plan.tokens, KEY_VALUE_HEADS * HEAD_SIZE), BF16),
            ],
            [WHOLE] * (2 * chips + len(far_kv)),
        )(*exchange(dq_pieces), *near_kv, *far_kv)
    )


def solution(mesh):
    n_seq, n_head = mesh.shape["seq"], mesh.shape["head"]
    fold = KEY_VALUE_HEADS // n_head
    assert n_head * fold == KEY_VALUE_HEADS and n_seq % fold == 0 and n_head % CORES == 0
    names = ("z", "y", "x", "core")
    planes = Mesh(mesh.devices.reshape(n_seq // fold, fold, n_head // CORES, CORES), names)
    rows = P(names, None)
    return jax.shard_map(
        body,
        mesh=planes,
        in_specs=(rows,) * 5 + (P(("x", "core"), ("z", "y")), P()),
        out_specs=(rows,) * 3,
        check_vma=False,
    )
```

```python
import functools
import math

import jax
import jax.numpy as jnp
from jax import lax
from jax.experimental import pallas as pl
from jax.experimental.pallas import tpu as pltpu
from jax.sharding import Mesh, PartitionSpec as P


HEAD_SIZE = 128
KEY_VALUE_HEADS = 8
QUERY_HEADS = 16
WIN = 5
GROUP = QUERY_HEADS // KEY_VALUE_HEADS
CORES = 2
KEY_TILE = 256
QUERY_TILE = 128
LANES = 128
PACK = 16
LOG2E = math.log2(math.e)
SCALE = 1.0 / math.sqrt(HEAD_SIZE)
BF16 = jnp.bfloat16
F32 = jnp.float32
CROSS = ("y", "x")
WHOLE = pl.BlockSpec(memory_space=pltpu.VMEM)
IN_HBM = pl.BlockSpec(memory_space=pltpu.HBM)
SCALARS = pl.BlockSpec(memory_space=pltpu.SMEM)
VMEM_BYTES = 16 * 1024 * 1024


def call(kernel, out_shape, in_specs, flops=0, moved=4 << 20, scratch=()):
    def placed(*refs):
        n_x = lax.axis_size("x")
        return kernel((lax.axis_index("y") * n_x + lax.axis_index("x"), lax.axis_index("core")), *refs)

    return pl.pallas_call(
        placed,
        out_shape=out_shape,
        in_specs=in_specs,
        out_specs=jax.tree.map(lambda _: WHOLE, out_shape),
        scratch_shapes=scratch,
        cost_estimate=pl.CostEstimate(flops=flops, bytes_accessed=moved, transcendentals=0),
        compiler_params=pltpu.CompilerParams(vmem_limit_bytes=VMEM_BYTES),
    )


def split3(x):
    hi = x.astype(BF16)
    rest = x - hi.astype(F32)
    mid = rest.astype(BF16)
    low = (rest - mid.astype(F32)).astype(BF16)
    return hi, mid, low


def round_up(n, to):
    return -(-n // to) * to


class Plan:
    def __init__(self, fold, n_x, tokens):
        self.fold, self.n_x, self.tokens = fold, n_x, tokens
        self.chips = fold * n_x
        self.kv_heads = KEY_VALUE_HEADS // self.chips
        self.q_heads = self.kv_heads * GROUP
        self.block = n_x * CORES * tokens
        self.q_rows = self.q_heads * tokens
        self.kv_rows = 2 * self.kv_heads * tokens
        self.aux_sent = round_up(3 * self.q_heads, PACK)
        self.aux = round_up(6 * self.q_heads, PACK)
        self.q_tiles = n_x * tokens // QUERY_TILE
        self.k_tiles = self.block // KEY_TILE
        assert self.k_tiles == 2

    def first_kv_head(self, chip):
        return ((chip % self.n_x) * self.fold + chip // self.n_x) * self.kv_heads


def columns(ref, head):
    return ref.at[:, pl.ds(pl.multiple_of(head * HEAD_SIZE, LANES), HEAD_SIZE)]


def padded_lanes(x):
    rows, width = x.shape
    if width == LANES:
        return x
    return jnp.concatenate([x, jnp.zeros((rows, LANES - width), x.dtype)], axis=1)


def padded_rows(terms, rows):
    have = sum(t.shape[0] for t in terms)
    if have < rows:
        terms = terms + [jnp.zeros((rows - have, LANES), BF16)]
    return jnp.concatenate(terms, axis=0)


def load(arrived, pairs):
    started = []
    for n, (source, target) in enumerate(pairs):
        size = target.shape[0] // 4
        parts = []
        for part in range(4):
            rows = pl.ds(part * size, size)
            copy = pltpu.make_async_copy(source.at[rows], target.at[rows], arrived.at[n, part])
            copy.start()
            parts.append(copy)
        started.append(parts)

    def wait_for(n):
        for copy in started[n]:
            copy.wait()

    return wait_for


def pack_kernel(plan, me, do_hbm, o_hbm, k_hbm, v_hbm, *refs):
    pieces, (do_ref, o_ref, k_ref, v_ref, delta_ref, arrived) = refs[: plan.chips], refs[plan.chips :]
    tokens = plan.tokens
    wait_for = load(arrived, ((do_hbm, do_ref), (o_hbm, o_ref), (k_hbm, k_ref), (v_hbm, v_ref)))
    wait_for(0)
    wait_for(1)
    sums = []
    for head in range(QUERY_HEADS):
        cols = slice(head * HEAD_SIZE, (head + 1) * HEAD_SIZE)
        product = do_ref[:, cols].astype(F32) * o_ref[:, cols].astype(F32)
        sums.append(jnp.sum(product, axis=1, keepdims=True))
    sums.append(jnp.zeros((tokens, LANES - QUERY_HEADS), F32))
    delta_ref[...] = padded_lanes(jnp.concatenate(sums, axis=1).T)
    wait_for(2)
    wait_for(3)
    for mask, out in enumerate(pieces):
        kv_head = plan.first_kv_head(me[0] ^ mask)
        terms = []
        for g in range(plan.q_heads):
            head = kv_head * GROUP + g
            out[g * tokens : (g + 1) * tokens, :] = columns(do_ref, head)[...]
            terms.extend(split3(delta_ref[pl.ds(head, 1), :]))
        for h in range(plan.kv_heads):
            at = plan.q_rows + h * tokens
            out[at : at + tokens, :] = columns(k_ref, kv_head + h)[...]
            at += plan.kv_heads * tokens
            out[at : at + tokens, :] = columns(v_ref, kv_head + h)[...]
        out[plan.q_rows + plan.kv_rows :, :] = padded_rows(terms, plan.aux_sent)


def pack_q_kernel(plan, me, own_hbm, *refs):
    own_ref, arrived = refs[-2:]
    above, pieces = refs[: -plan.chips - 2], refs[-plan.chips - 2 : -2]
    tokens = plan.tokens
    wait_for = load(arrived, ((own_hbm, own_ref),))
    for level, ref in reversed(list(enumerate((own_ref,) + above))):
        if level == 0:
            wait_for(0)
        for mask, out in enumerate(pieces):
            first = plan.first_kv_head(me[0] ^ mask) * GROUP
            for g in range(plan.q_heads):
                at = level * plan.q_rows + g * tokens
                out[at : at + tokens, :] = columns(ref, first + g)[...]


def stack_kernel(me, *refs):
    pieces, out = refs[:-1], refs[-1]
    rows = pieces[0].shape[0]
    for n, piece in enumerate(pieces):
        out[n * rows : (n + 1) * rows, :] = piece[...]


def assemble_kernel(plan, me, lse_ref, *refs):
    pieces, (do_out, kv_out) = refs[:-2], refs[-2:]
    tokens, split = plan.tokens, plan.q_rows + plan.kv_rows
    for mask, piece in enumerate(pieces):
        chip = me[0] ^ mask
        chunk = (chip % plan.n_x) * CORES + me[1]
        do_out[chip, : plan.q_rows, :] = piece[: plan.q_rows, :]
        kv_out[chip] = piece[plan.q_rows : split, :]
        terms = [piece[split : split + 3 * plan.q_heads, :]]
        for g in range(plan.q_heads):
            if tokens == LANES:
                lanes = pl.ds(pl.multiple_of(chunk * LANES, LANES), LANES)
                row = lse_ref[mask // plan.n_x, pl.ds(g, 1), lanes]
            else:
                row = lse_ref[mask // plan.n_x, chunk, pl.ds(g, 1), :]
            terms.extend(split3(row))
        do_out[chip, plan.q_rows :, :] = padded_rows(terms, plan.aux)


def merge_kernel(groups, me, keep_ref, given_ref, *outs):
    for group, out in zip(groups, outs):
        rows = keep_ref.shape[1]
        for n, mask in enumerate(group):
            chip = me[0] ^ mask
            out[n * rows : (n + 1) * rows, :] = (keep_ref[chip] + given_ref[chip].astype(F32)).astype(BF16)


def lane_row(parts, tokens):
    row = parts[0]
    lane = lax.broadcasted_iota(jnp.int32, row.shape, 1)
    for n, part in enumerate(parts[1:], 1):
        row = jnp.where(lane >= n * tokens, pltpu.roll(part, n * tokens, 1), row)
    return row


def role_kernel(plan, level, has_dq, has_dkv, last, me, code_ref, mine_ref, sib_ref, *refs):
    refs = list(refs)
    q_pieces = [refs.pop(0) for _ in range(plan.chips)]
    do_ref = refs.pop(0)
    dq_in = refs.pop(0) if has_dq else None
    dkv_in = refs.pop(0) if has_dkv else None
    dq_out, dkv_outs, (kv_ref, q_ref, dq_sum, dkv_sum) = refs[0], refs[1:-4], refs[-4:]
    dq_ref = dq_out if dq_out.dtype == F32 else dq_sum
    dkv_ref = dkv_sum if last else dkv_outs[0]
    core = me[1]
    tokens, n_x, fold = plan.tokens, plan.n_x, plan.fold
    q_per = QUERY_TILE // tokens
    k_per = KEY_TILE // tokens
    kv_ref[core] = mine_ref[...]
    kv_ref[1 - core] = sib_ref[...]
    dkv_ref[...] = dkv_in[...] if has_dkv else jnp.zeros_like(dkv_ref)
    dq_ref[...] = dq_in[...] if has_dq else jnp.zeros_like(dq_ref)
    for mask, piece in enumerate(q_pieces):
        q_ref[me[0] ^ mask] = piece[level * plan.q_rows : (level + 1) * plan.q_rows, :]

    def q_start(q_in):
        return (q_in * q_per * CORES + core) * tokens

    def q_end(q_in):
        return ((q_in * q_per + q_per - 1) * CORES + core) * tokens + tokens - 1

    rows_by_rows = (((1,), (1,)), ((), ()))

    def row(query_block, q_in, key_block, k_tiles, code, masked):
        q_chip = query_block * n_x + q_in * q_per
        tile = query_block * plan.q_tiles + q_in

        def q_part(ref, g):
            return [ref[q_chip + n, g * tokens : (g + 1) * tokens, :] for n in range(q_per)]

        def k_place(k_in):
            return [
                (n % CORES, key_block * n_x + k_in * (k_per // CORES) + n // CORES) for n in range(k_per)
            ]

        def k_part(which, h, k_in):
            at = (which * plan.kv_heads + h) * tokens
            return jnp.concatenate([kv_ref[c, chip, at : at + tokens, :] for c, chip in k_place(k_in)], axis=0)

        groups = [do_ref[q_chip + n, plan.q_rows :, :].astype(F32) for n in range(q_per)]

        def aux(which, g):
            at = (which * plan.q_heads + g) * 3
            return lane_row([a[at : at + 1] + a[at + 1 : at + 2] + a[at + 2 : at + 3] for a in groups], tokens)

        queries = []
        for h in range(plan.kv_heads):
            heads = range(h * GROUP, (h + 1) * GROUP)
            q2 = jnp.concatenate([r for g in heads for r in q_part(q_ref, g)], axis=0)
            do2 = jnp.concatenate([r for g in heads for r in q_part(do_ref, g)], axis=0)
            delta = jnp.concatenate([aux(0, g) for g in heads], axis=1)
            lse = jnp.concatenate([aux(1, g) for g in heads], axis=1) * LOG2E
            queries.append((q2, do2, delta, lse))
        units = [(h, k_in) for k_in in k_tiles for h in range(plan.kv_heads)]

        def front(unit):
            h, k_in = unit
            q2, do2, _, _ = queries[h]
            k, v = k_part(0, h, k_in), k_part(1, h, k_in)
            scores = lax.dot_general(k, q2, rows_by_rows, preferred_element_type=F32)
            dprobs = lax.dot_general(v, do2, rows_by_rows, preferred_element_type=F32)
            return k, scores, dprobs

        def back(unit, ready):
            h, k_in = unit
            q2, do2, delta, lse = queries[h]
            k, scores, dprobs = ready
            probs = jnp.exp2(scores * (SCALE * LOG2E) - lse)
            if masked:
                key_at = lax.broadcasted_iota(jnp.int32, probs.shape, 0) + k_in * KEY_TILE
                lane = lax.broadcasted_iota(jnp.int32, probs.shape, 1) % QUERY_TILE
                query_at = q_start(q_in) + lane % tokens + (lane // tokens) * (CORES * tokens)
                ahead = key_at - query_at
                allowed = jnp.where(code == 2, ahead, 1 - ahead) <= 0
                probs = jnp.where(allowed, probs, 0.0)
            dscores = (probs * (dprobs - delta) * SCALE).astype(BF16)
            dv = jnp.dot(probs.astype(BF16), do2, preferred_element_type=F32)
            dk = jnp.dot(dscores, q2, preferred_element_type=F32)
            for n, (c, chip) in enumerate(k_place(k_in)):
                rows = slice(n * tokens, (n + 1) * tokens)
                at = h * tokens
                dkv_ref[c, chip, at : at + tokens, :] += dk[rows]
                at += plan.kv_heads * tokens
                dkv_ref[c, chip, at : at + tokens, :] += dv[rows]
            return jnp.dot(k.T, dscores, preferred_element_type=F32)

        ready = front(units[0])
        for n, unit in enumerate(units):
            following = front(units[n + 1]) if n + 1 < len(units) else None
            dq_ref[tile, unit[0]] += back(unit, ready)
            ready = following

    def step(index, carry):
        q_in = index % plan.q_tiles
        rest = index // plan.q_tiles
        key_block = rest % fold
        query_block = rest // fold
        code = code_ref[query_block, key_block]
        q_first, q_last = q_start(q_in), q_end(q_in)
        every = tuple(range(plan.k_tiles))
        below = (q_last < (plan.k_tiles - 1) * KEY_TILE) & (code == 2)
        above = (q_first >= KEY_TILE - 1) & (code == 3)

        @pl.when(code == 1)
        def _():
            row(query_block, q_in, key_block, every, code, False)

        @pl.when(below | above)
        def _():
            row(query_block, q_in, key_block, (jnp.where(below, 0, plan.k_tiles - 1),), code, True)

        @pl.when((code >= 2) & jnp.logical_not(below | above))
        def _():
            row(query_block, q_in, key_block, every, code, True)

        return carry

    lax.fori_loop(0, fold * fold * plan.q_tiles, step, 0)
    if dq_out.dtype != F32:
        dq_out[...] = dq_ref[...].astype(dq_out.dtype)
    if last:
        keep, give = dkv_outs
        keep[...] = dkv_ref[core]
        give[...] = dkv_ref[1 - core].astype(BF16)


def finish_kernel(plan, has_far, me, dq_ref, *refs):
    refs = list(refs)
    far_ref = refs.pop(0) if has_far else None
    pieces, rows_ref = refs[:-1], refs[-1]
    tokens = plan.tokens
    q_per = QUERY_TILE // tokens
    for tile in range(dq_ref.shape[0]):
        for h in range(plan.kv_heads):
            total = dq_ref[tile, h]
            if has_far:
                total = total + far_ref[tile, h].astype(F32)
            turned = total.T.astype(BF16)
            for g in range(GROUP):
                for n in range(q_per):
                    at = (h * GROUP + g) * tokens
                    source = g * QUERY_TILE + n * tokens
                    rows_ref[tile * q_per + n, at : at + tokens, :] = turned[source : source + tokens]
    for mask, out in enumerate(pieces):
        out[...] = rows_ref[me[0] ^ mask]


def unpack_kernel(plan, levels, me, *refs):
    refs = list(refs)
    direct, by_way = routes(plan.chips)
    dq_pieces = [refs.pop(0) for _ in range(plan.chips)]
    near = [refs.pop(0) for _ in range(plan.chips)]
    far = {mask: [] for mask in range(plan.chips)}
    for _ in range(levels - 1):
        for mask in direct:
            far[mask].append((refs.pop(0), 0))
        both = refs.pop(0)
        for n, mask in enumerate(by_way):
            far[mask].append((both, n * plan.kv_rows))
    dq_ref, dk_ref, dv_ref = refs
    tokens = plan.tokens
    for mask in range(plan.chips):
        kv_head = plan.first_kv_head(me[0] ^ mask)
        for g in range(plan.q_heads):
            columns(dq_ref, kv_head * GROUP + g)[...] = dq_pieces[mask][g * tokens : (g + 1) * tokens, :]
        total = near[mask][...]
        if far[mask]:
            total = total.astype(F32)
            for ref, at in far[mask]:
                total = total + ref[at : at + plan.kv_rows, :].astype(F32)
            total = total.astype(BF16)
        for h in range(plan.kv_heads):
            columns(dk_ref, kv_head + h)[...] = total[h * tokens : (h + 1) * tokens]
            at = (plan.kv_heads + h) * tokens
            columns(dv_ref, kv_head + h)[...] = total[at : at + tokens]


def routes(chips):
    by_way = [mask for mask in range(chips) if mask.bit_count() == 1]
    return [mask for mask in range(chips) if mask not in by_way], by_way


def send_in_plane(piece, mask, chips):
    if mask == 0:
        return piece
    return lax.ppermute(piece, CROSS, [(i, i ^ mask) for i in range(chips)])


def exchange(pieces):
    return [send_in_plane(piece, mask, len(pieces)) for mask, piece in enumerate(pieces)]


def swap(value):
    return lax.ppermute(value, "core", [(0, 1), (1, 0)])


def along(value, planes, steps):
    pairs = [(i, i + steps) for i in range(planes) if 0 <= i + steps < planes]
    return lax.ppermute(value, "z", pairs)


def query_levels(level, reach):
    return [d - level for d in (2 * level, 2 * level - 1) if 0 <= d <= reach]


def plane_logsum(logsum, plan, y, core):
    blocks = [logsum]
    for mask in range(1, plan.fold):
        blocks.append(lax.ppermute(logsum, "y", [(i, i ^ mask) for i in range(plan.fold)]))
    mine = jnp.stack(blocks)
    other = swap(mine)
    both = jnp.where(core == 0, jnp.concatenate([mine, other], axis=1), jnp.concatenate([other, mine], axis=1))
    lse = lax.dynamic_slice_in_dim(both, y * plan.q_heads, plan.q_heads, axis=1)
    if plan.tokens == LANES:
        return lse
    lse = lse.reshape(plan.fold, plan.q_heads, plan.n_x * CORES, plan.tokens).transpose(0, 2, 1, 3)
    return jnp.pad(lse, ((0, 0), (0, 0), (0, 0), (0, LANES - plan.tokens)))


def body(queries, output_gradient, outputs, key_vectors, values, logsum, pair_list):
    planes, fold, n_x = (lax.axis_size(a) for a in ("z", "y", "x"))
    plan = Plan(fold, n_x, queries.shape[0])
    chips = plan.chips
    reach = -(-(WIN - 1) // fold)
    z, y, core = (lax.axis_index(a) for a in ("z", "y", "core"))

    def like(rows):
        return jax.ShapeDtypeStruct((rows, LANES), BF16)

    def stacked(rows, dtype=BF16):
        return jax.ShapeDtypeStruct((chips, rows, LANES), dtype)

    kept = functools.partial(pltpu.with_memory_space_constraint, memory_space=pltpu.HBM)
    raw = [queries]
    for _ in range(1, reach // 2 + 1):
        raw.append(along(raw[-1], planes, -1))

    lse = plane_logsum(logsum, plan, y, core)
    arrays = (output_gradient, outputs, key_vectors, values)
    pieces = call(
        functools.partial(pack_kernel, plan),
        [like(plan.q_rows + plan.kv_rows + plan.aux_sent)] * chips,
        [IN_HBM] * len(arrays),
        scratch=[pltpu.VMEM(a.shape, a.dtype) for a in arrays]
        + [pltpu.VMEM((LANES, LANES), F32), pltpu.SemaphoreType.DMA((len(arrays), 4))],
    )(*map(kept, arrays))
    do_own, kv_own = call(
        functools.partial(assemble_kernel, plan),
        [stacked(plan.q_rows + plan.aux), stacked(plan.kv_rows)],
        [WHOLE] * (chips + 1),
    )(lse, *exchange(pieces))

    up = [kv_own]
    for _ in range(1, (reach + 1) // 2 + 1):
        up.append(along(up[-1], planes, 1))
    far_do = [do_own]
    for _ in range(1, reach // 2 + 1):
        far_do.append(along(far_do[-1], planes, -1))
    q_pieces = exchange(
        call(
            functools.partial(pack_q_kernel, plan),
            [like(len(raw) * plan.q_rows)] * chips,
            [IN_HBM] + [WHOLE] * (len(raw) - 1),
            scratch=[pltpu.VMEM(queries.shape, BF16), pltpu.SemaphoreType.DMA((1, 4))],
        )(kept(queries), *raw[1:]),
    )
    up = [(kv, swap(kv)) for kv in up]

    grad_q = [None] * len(raw)
    near_kv, far_kv = None, []
    dq_shape = (fold * plan.q_tiles, plan.kv_heads, HEAD_SIZE, GROUP * QUERY_TILE)
    dkv_shape = (CORES, chips, plan.kv_rows, LANES)
    inside = jnp.arange(fold, dtype=jnp.int32)
    cases = [(i, j) for i in range(len(up)) for j in query_levels(i, reach)]
    query_blocks = (z + jnp.array([j for _, j in cases], jnp.int32)[:, None]) * fold + inside
    key_blocks = (z - jnp.array([i for i, _ in cases], jnp.int32)[:, None]) * fold + inside
    listed = pair_list[:, :, None, None, None]
    hit = (listed[:, 0] == query_blocks[:, :, None]) & (listed[:, 1] == key_blocks[:, None, :])
    codes = jnp.sum(jnp.where(hit, listed[:, 2] + 1, 0), axis=0).astype(jnp.int32)
    direct, by_way = routes(chips)
    for i, (mine, sibling) in enumerate(up):
        levels = query_levels(i, reach)
        carried = None
        for j in levels:
            has_dq, last = grad_q[j] is not None, j == levels[-1]
            done = j and j not in query_levels(i + 1, reach)
            dkv_outs = (
                [stacked(plan.kv_rows, F32), stacked(plan.kv_rows)]
                if last
                else [jax.ShapeDtypeStruct(dkv_shape, F32)]
            )
            given = [g for g in (grad_q[j], carried) if g is not None]
            grad_q[j], *dkv = call(
                functools.partial(role_kernel, plan, j, has_dq, carried is not None, last),
                [jax.ShapeDtypeStruct(dq_shape, BF16 if done else F32)] + dkv_outs,
                [SCALARS] + [WHOLE] * (3 + chips + len(given)),
                flops=10 * fold * fold * plan.q_heads * plan.block * plan.block * HEAD_SIZE // CORES,
                scratch=[
                    pltpu.VMEM(dkv_shape, BF16),
                    pltpu.VMEM((chips, plan.q_rows, LANES), BF16),
                    pltpu.VMEM(dq_shape, F32),
                    pltpu.VMEM(dkv_shape, F32),
                ],
            )(codes[cases.index((i, j))], mine, sibling, *q_pieces, far_do[j], *given)
            carried = dkv[0]
        keep, give = dkv
        groups = [direct] + [[m] for m in by_way] if i else [[m] for m in range(chips)]
        merged = call(
            functools.partial(merge_kernel, groups), [like(len(group) * plan.kv_rows) for group in groups], [WHOLE] * 2
        )(keep, swap(give))
        if i == 0:
            near_kv = exchange(merged)
            continue
        first = along(merged[0], planes, -i)
        for n, mask in enumerate(direct):
            piece = first[n * plan.kv_rows : (n + 1) * plan.kv_rows]
            far_kv.append(send_in_plane(piece, mask, chips))
        pair = [send_in_plane(p, m, chips) for p, m in zip(merged[1:], by_way)]
        both = call(stack_kernel, like(len(by_way) * plan.kv_rows), [WHOLE] * len(by_way))(*pair)
        far_kv.append(along(both, planes, -i))

    def plus(part, far):
        return part if far is None else (part.astype(F32) + far.astype(F32)).astype(BF16)

    far_q = None
    for level in range(len(grad_q) - 1, 0, -1):
        far_q = along(plus(grad_q[level], far_q), planes, 1)
    dq_pieces = call(
        functools.partial(finish_kernel, plan, far_q is not None),
        [like(plan.q_rows)] * chips,
        [WHOLE] + [WHOLE] * (far_q is not None),
        scratch=[pltpu.VMEM((chips, plan.q_rows, LANES), BF16)],
    )(grad_q[0], *([] if far_q is None else [far_q]))
    return tuple(
        call(
            functools.partial(unpack_kernel, plan, len(up)),
            [
                jax.ShapeDtypeStruct((plan.tokens, QUERY_HEADS * HEAD_SIZE), BF16),
                jax.ShapeDtypeStruct((plan.tokens, KEY_VALUE_HEADS * HEAD_SIZE), BF16),
                jax.ShapeDtypeStruct((plan.tokens, KEY_VALUE_HEADS * HEAD_SIZE), BF16),
            ],
            [WHOLE] * (2 * chips + len(far_kv)),
        )(*exchange(dq_pieces), *near_kv, *far_kv)
    )


def solution(mesh):
    n_seq, n_head = mesh.shape["seq"], mesh.shape["head"]
    fold = KEY_VALUE_HEADS // n_head
    assert n_head * fold == KEY_VALUE_HEADS and n_seq % fold == 0 and n_head % CORES == 0
    names = ("z", "y", "x", "core")
    planes = Mesh(mesh.devices.reshape(n_seq // fold, fold, n_head // CORES, CORES), names)
    rows = P(names, None)
    return jax.shard_map(
        body,
        mesh=planes,
        in_specs=(rows,) * 5 + (P(("x", "core"), ("z", "y")), P()),
        out_specs=(rows,) * 3,
        check_vma=False,
    )
```
